512 devices in a mesh: row: 8 (over y_lo, core), col: 64 (over z, y_hi, x).
Axes of the slice: x: 4, y: 8 (y_hi: 2, y_lo: 4; y = y_hi * 4 + y_lo), z: 8, core: 2. Of those that a mesh axis runs over, the one named last changes fastest.
Arguments:
- first_factor_strip: bfloat16 [4096, 8192], P('row', 'col'), may hold values from -16 to 16
- second_factor_strip: bfloat16 [8192, 24576], P('row', 'col'), may hold values from -0.0625 to 0.0625
- first_factor_support: int32 [32, 64], P('row', 'col'), may hold values 0 or 1
- second_factor_support: int32 [64, 192], P('row', 'col'), may hold values 0 or 1
- retained_blocks: int32 [32, 192], P('row', 'col'), may hold values 0 or 1
- target_bands: int32 [8, 64, 12, 1], P('row', 'col'), may hold values from 0 to 7; in each aligned block of 12 rows (0 to 11, 12 to 23, ..., all dimensions but the last counted through in order) at most 2 rows name the same one
Outputs:
- stochastic_result: bfloat16 [4096, 24576], P('row', 'col')
- redistributed_result: bfloat16 [16384, 8192], P('row', 'col')
The draws below stay inside these ranges and needn't reach their ends.
Inputs may be any that keep to these rules, and one draw needn't show every extreme that they name: `target_bands`: among the tiles of one block no destination is named more than 2 times, and in some block one destination is named exactly 2 times.
All inputs are finite; a program needn't handle non-finite values. No bound on the sum of `first_factor_support` or of `second_factor_support` or of `retained_blocks` on one device may be relied on, other than what follows from the above.
Results may differ from the reference program's by a relative error of at most 0.001.
Values may be sent and summed in bfloat16 or wider, within the bound.
A program may use at most 64 MiB of HBM per device.

```python
import math
import jax
import jax.numpy as jnp
import numpy as np

BLOCK_EDGE = 128
BLOCK_LINES = 4
BLOCK_VERTICALS = 3
KT = 1
HORIZONTAL_BANDS = 8
VERTICAL_BANDS = 64
NR = 4096
NC = 24576
K = 8192
BERTH_LIMIT = 2


def draw_first_factor_strip(key, part):
    first, second = jax.random.split(key)
    ramp = (3.0 ** (jnp.arange(NR).astype(jnp.float32) / max(NR - 1, 1)))[:, None]
    base = jnp.clip(jax.random.normal(first, (NR, K), jnp.float32), -5.0, 5.0)
    rough = jnp.exp(jax.random.uniform(second, (NR, 1), jnp.float32, 0.0, math.log(3.0)))
    return (base * ramp * rough / 3.0).astype(jnp.bfloat16)


def touch_ends(values, own_key, smallest, largest):
    longest = values.shape.index(max(values.shape))
    spots = []
    for shift in (0, 1):
        where = [jax.random.randint(jax.random.fold_in(own_key, axis), (), 0, length) for axis, length in enumerate(values.shape)]
        where[longest] = (where[longest] + shift) % values.shape[longest]
        spots.append(tuple(where))
    return values.at[spots[0]].set(smallest).at[spots[1]].set(largest)


def levels(own_key, dims, cuts, least, high):
    factor_of = 1.0
    for dim, parts in cuts:
        heights = jax.random.uniform(jax.random.fold_in(jax.random.fold_in(own_key, 6), dim), (parts,), jnp.float32, least / len(cuts), high / len(cuts))
        factor_of = factor_of * jnp.repeat(jnp.exp(heights), dims[dim] // parts).reshape((-1,) + (1,) * (len(dims) - 1 - dim))
    return factor_of


def deal_out(key, own, number, rows, number_of, top, reach, skew):
    order = jax.random.permutation(key, number_of)
    packed, usual = shares(number_of, rows * top, reach, skew, True), shares(number_of, rows * top, reach, skew, False)
    places = jnp.arange(number_of)

    def named(sizes, offset_by):
        used = int((sizes > 0).sum())
        fixed = max(1, used // 4)
        passed = fixed + (places - fixed + offset_by * (used - fixed)) % max(1, number_of - fixed)
        return jnp.zeros((number_of,), jnp.int32).at[order[jnp.where(places < fixed, places, passed)]].set(jnp.asarray(sizes, jnp.int32))

    sizes = jnp.where(number % 4 == 0, named(packed, number // 4), named(usual, number - number // 4 - 1))
    mixed = jax.random.permutation(jax.random.fold_in(own, 3), number_of)
    donor, taker = mixed[0:number_of // 2 * 2:2], mixed[1:number_of // 2 * 2:2]
    margin = jnp.minimum(sizes[donor] - 1, reach - sizes[taker]) // 2
    margin = jnp.where((donor == order[0]) | (taker == order[0]) | (sizes[taker] == 0), 0, jnp.maximum(margin, 0))
    passed = jax.random.randint(jax.random.fold_in(own, 4), (number_of // 2,), 0, 1 << 20) % (margin + 1)
    sizes = sizes.at[donor].add(-passed).at[taker].add(passed)
    items = jnp.searchsorted(jnp.cumsum(sizes), jnp.arange(rows * top), side="right").astype(jnp.int32)
    listing = items.reshape(top, rows).T
    listing = listing[jax.random.permutation(jax.random.fold_in(own, 1), rows)]
    offset_by = jax.random.randint(jax.random.fold_in(own, 2), (rows, 1), 0, top)
    return jnp.take_along_axis(listing, (jnp.arange(top)[None, :] + offset_by) % top, axis=1)


def shares(number_of, total, reach, lean, full):
    weights = [(1 << 20) // math.isqrt(rank ** lean) + 1 for rank in range(1, number_of + 1)]
    largest = reach if full else min(reach, max(-(-total // number_of), total * weights[0] // sum(weights)))
    least = 1 if total - largest >= number_of - 1 else 0
    holding, surplus = [largest] + [least] * (number_of - 1), total - largest - least * (number_of - 1)
    while surplus > 0:
        candidates = [i for i in range(1, number_of) if holding[i] < largest] or [i for i in range(1, number_of) if holding[i] < reach]
        mass, budget = sum([weights[i] for i in candidates]), surplus
        for i in candidates:
            more = min(reach - holding[i], max(1, budget * weights[i] // mass), surplus)
            holding[i] = holding[i] + more
            surplus = surplus - more
    return np.array(holding)


def noise(key, extent, scale, limit, shards=(), held_as=jnp.bfloat16):
    values = jax.random.normal(key, extent, jnp.float32) * scale
    if len(shards) > 0:
        values = levels(key, extent, shards, -0.22, 0.18) * values
    return jnp.clip(values, min=-limit, max=limit).astype(held_as)


def setup_inputs(seed: int = 0) -> dict:
    key_of = jax.random.split(jax.random.key(seed), 7)
    first_factor_strip = draw_first_factor_strip(jax.random.fold_in(key_of[6], 71), 0)
    second_factor_strip = noise(key_of[1], (K, NC), K ** -0.5, 0.0625, ((0, 8), (1, 64)))
    first_factor_support = touch_ends((jax.random.randint(key_of[2], (BLOCK_LINES * HORIZONTAL_BANDS, KT * VERTICAL_BANDS), 0, 8) < 5).astype(jnp.int32), jax.random.fold_in(key_of[2], 1), 0, 1)
    second_factor_support = touch_ends((jax.random.randint(key_of[3], (KT * VERTICAL_BANDS, BLOCK_VERTICALS * VERTICAL_BANDS), 0, 8) < 5).astype(jnp.int32), jax.random.fold_in(key_of[3], 1), 0, 1)
    retained_blocks = touch_ends((jax.random.randint(key_of[4], (BLOCK_LINES * HORIZONTAL_BANDS, BLOCK_VERTICALS * VERTICAL_BANDS), 0, 8) < 7).astype(jnp.int32), jax.random.fold_in(key_of[4], 1), 0, 1)
    target_bands_keys = jax.random.split(jax.random.fold_in(key_of[5], 1), HORIZONTAL_BANDS * VERTICAL_BANDS * (BLOCK_LINES * BLOCK_VERTICALS) // (BLOCK_LINES * BLOCK_VERTICALS))
    target_bands_turns = jax.random.permutation(jax.random.fold_in(key_of[5], 3), HORIZONTAL_BANDS * VERTICAL_BANDS * (BLOCK_LINES * BLOCK_VERTICALS) // (BLOCK_LINES * BLOCK_VERTICALS))
    target_bands = jax.vmap(lambda own, number: deal_out(jax.random.fold_in(key_of[5], 2), own, number, BLOCK_LINES * BLOCK_VERTICALS, HORIZONTAL_BANDS, 1, BERTH_LIMIT, 2))(target_bands_keys, target_bands_turns).reshape((HORIZONTAL_BANDS, VERTICAL_BANDS, BLOCK_LINES * BLOCK_VERTICALS, 1))
    return {"first_factor_strip": first_factor_strip, "second_factor_strip": second_factor_strip, "first_factor_support": first_factor_support, "second_factor_support": second_factor_support, "retained_blocks": retained_blocks, "target_bands": target_bands}


def squaring_pass(values, pattern):
    row_tiles, col_tiles = pattern.shape
    shaped = values.reshape(row_tiles, BLOCK_EDGE, col_tiles, BLOCK_EDGE)
    return (shaped * pattern[:, None, :, None].astype(values.dtype)).reshape(values.shape)


def reference(first_factor_strip, second_factor_strip, first_factor_support, second_factor_support, retained_blocks, target_bands):
    a_eff = squaring_pass(first_factor_strip, first_factor_support)
    b_eff = squaring_pass(second_factor_strip, second_factor_support)
    multiplied_blocks = jnp.dot(a_eff, b_eff, preferred_element_type=jnp.float32)
    powered_blocks = squaring_pass(multiplied_blocks * multiplied_blocks, retained_blocks)
    col_mean = jnp.sum(powered_blocks, axis=0) / NR
    stochastic_result = (powered_blocks / (col_mean + 1e-5)).astype(jnp.bfloat16)
    tile_count = BLOCK_LINES * BLOCK_VERTICALS
    tile_stack = stochastic_result.reshape(HORIZONTAL_BANDS, BLOCK_LINES, BLOCK_EDGE, VERTICAL_BANDS, BLOCK_VERTICALS, BLOCK_EDGE)
    tile_stack = tile_stack.transpose(0, 3, 1, 4, 2, 5).reshape(HORIZONTAL_BANDS, VERTICAL_BANDS, tile_count, BLOCK_EDGE, BLOCK_EDGE)
    targets = target_bands[..., 0]
    same_target = targets[..., :, None] == targets[..., None, :]
    earlier = jnp.arange(tile_count)[None, :] < jnp.arange(tile_count)[:, None]
    slot_rank = jnp.sum((same_target & earlier).astype(jnp.int32), axis=-1).astype(jnp.int32)
    position = targets * BERTH_LIMIT + slot_rank
    selector = (position[..., None] == jnp.arange(HORIZONTAL_BANDS * BERTH_LIMIT)[None, None, None, :]).astype(jnp.float32)
    selector = selector.reshape(HORIZONTAL_BANDS, VERTICAL_BANDS, tile_count, HORIZONTAL_BANDS, BERTH_LIMIT)
    positioned_blocks = jnp.einsum('ijtds,ijtab->disajb', selector, tile_stack.astype(jnp.float32))
    redistributed_result = positioned_blocks.reshape(HORIZONTAL_BANDS * HORIZONTAL_BANDS * BERTH_LIMIT * BLOCK_EDGE, VERTICAL_BANDS * BLOCK_EDGE).astype(jnp.bfloat16)
    return stochastic_result, redistributed_result
```

```python
import functools
import heapq

import jax
import jax.numpy as jnp
from jax import lax
from jax.experimental import pallas as pl
from jax.experimental.pallas import tpu as pltpu
from jax.sharding import PartitionSpec as P

MESH = pl.DeviceIdType.MESH
EDGE = 128
OWN, PARTNER = 0, 1
PARTS = {"full": (0, 512), "top": (0, 256), "bot": (256, 256)}
CHUNKS = ((0, 256), (256, 768))
PARTNER_READY = 13.0
BLOCK_US, HOP_US = 2.82, 1.8


def build_messages():
    msgs = []

    def add(axis, sign, dz, half, dx, part, level):
        came = (dz - sign, half, dx, part) if axis == "z" else (dz, half, dx - sign, part)
        msgs.append({"axis": axis, "sign": sign, "out": (dz, half, dx, part), "in": came, "level": level})

    for sign in (1, -1):
        add("x", sign, 0, OWN, 0, "full", 0)
    for sign in (1, -1):
        add("x", sign, 0, OWN, -sign, "top" if sign > 0 else "bot", 0)
    for dx in (0, -1, 1, 2):
        for step in range(4):
            for sign in (1, -1):
                part = "full" if step < 3 else ("top" if sign > 0 else "bot")
                add("z", sign, -sign * step, OWN, dx, part, 2)
    for step in range(4):
        for sign in (1, -1):
            part = "full" if step < 3 else ("top" if sign > 0 else "bot")
            add("z", sign, -sign * step, PARTNER, 0, part, 1)
    for dz in (0, -1, 1, -2, 2, -3, 3, 4):
        for sign in (1, -1):
            add("x", sign, dz, PARTNER, 0, "full", 1)
        for sign in (1, -1):
            add("x", sign, dz, PARTNER, -sign, "top" if sign > 0 else "bot", 1)
    return msgs


def halves(block):
    dz, half, dx, part = block
    key = (dz % 8, half, dx % 4)
    return {key + ("top",), key + ("bot",)} if part == "full" else {key + (part,)}


def plan(msgs):
    source = {}
    for k, m in enumerate(msgs):
        for h in halves(m["in"]):
            source[h] = k
    needs = [{source[h] for h in halves(m["out"]) if h in source} for m in msgs]
    ready_at = {}
    free = {("x", 1): 0.0, ("x", -1): 0.0, ("z", 1): 0.0, ("z", -1): 0.0}
    arrived, order, done = {}, [], set()
    heap = []
    for k, m in enumerate(msgs):
        if not needs[k]:
            heapq.heappush(heap, (PARTNER_READY if m["out"][1] == PARTNER else 0.0, m["level"], k))
    waited = set()
    events = []
    left = {k: set(n) for k, n in enumerate(needs)}
    partner_waited = False
    while heap:
        t, level, k = heapq.heappop(heap)
        m = msgs[k]
        link = (m["axis"], m["sign"])
        begin = max(t, free[link])
        size = PARTS[m["out"][3]][1] / 512 * BLOCK_US
        free[link] = begin + size
        arrived[k] = begin + size + HOP_US
        events.append((t, 1, k))
        for j, n in left.items():
            if k in n:
                n.discard(k)
                ready_at[j] = max(ready_at.get(j, 0.0), arrived[k])
                if not n:
                    heapq.heappush(heap, (ready_at[j], msgs[j]["level"], j))
    steps = []
    for t, _, k in events:
        for n in sorted(needs[k], key=lambda i: arrived[i]):
            if n not in waited:
                waited.add(n)
                steps.append((t, "wait", n))
        if msgs[k]["out"][1] == PARTNER and not partner_waited:
            partner_waited = True
            steps.append((t, "partner", 0))
        steps.append((t, "start", k))
    for k in sorted(arrived, key=lambda i: arrived[i]):
        if k not in waited:
            waited.add(k)
            steps.append((arrived[k], "wait", k))
    steps.sort(key=lambda s: s[0])
    return steps


def kernel(
    a_ref, b_ref, asup_ref, bsup_ref, keep_ref, band_ref,
    out_ref, moved_ref,
    a_all, b_all, acc, tiles, normal, outgoing, sums, slot_of, filled,
    a_send, a_recv, b_send, b_recv, s_send, s_recv, h_send, h_recv, c_send, c_recv, r_send, r_recv, local_sem,
):
    row, col = lax.axis_index("row"), lax.axis_index("col")
    y, core = row // 2, row % 2
    z, yh, x = col // 8, (col // 4) % 2, col % 4
    msgs = build_messages()
    steps = plan(msgs)

    def row_peer(k):
        py = (3 - y, (y + 2) % 4, y + 1 - 2 * (y % 2), y)[3 - k // 2]
        pc = 1 - core if k % 2 else core
        return py * 2 + pc

    def col_at(dz, dx, half):
        h = yh if half == OWN else 1 - yh
        return ((z + dz + 8) % 8) * 8 + h * 4 + (x + dx + 4) % 4

    across = ((y + 2) % 4) * 2 + core
    neighbours = [(row, col_at(0, 1, OWN)), (row, col_at(0, -1, OWN)), (row, col_at(1, 0, OWN)), (row, col_at(-1, 0, OWN))]
    neighbours += [(row_peer(k), col) for k in range(1, 8)]
    neighbours.append((across, col_at(0, 0, PARTNER)))

    barrier = pltpu.get_barrier_semaphore()
    for device in neighbours:
        pl.semaphore_signal(barrier, inc=1, device_id=device, device_id_type=MESH)

    for r in range(4):
        rows = pl.ds(r * EDGE, EDGE)
        tile = a_ref[rows, :]
        a_all[z, yh, x, rows, :] = jnp.where(asup_ref[r, 0] != 0, tile, jnp.zeros_like(tile))
    for r in range(8):
        for c in range(3):
            rows, cols = pl.ds(r * EDGE, EDGE), pl.ds(c * EDGE, EDGE)
            tile = b_ref[rows, cols]
            b_all[row, rows, cols] = jnp.where(bsup_ref[r, c] != 0, tile, jnp.zeros_like(tile))

    pl.semaphore_wait(barrier, len(neighbours))

    def block(spec):
        dz, half, dx, part = spec
        first, count = PARTS[part]
        h = yh if half == OWN else 1 - yh
        return a_all.at[(z + dz + 8) % 8, h, (x + dx + 4) % 4, pl.ds(first, count), :]

    def a_copy(k, spec):
        m = msgs[k]
        to = col_at(m["sign"], 0, OWN) if m["axis"] == "z" else col_at(0, m["sign"], OWN)
        return pltpu.make_async_remote_copy(
            src_ref=block(spec), dst_ref=block(spec), send_sem=a_send.at[k], recv_sem=a_recv.at[k],
            device_id=(row, to), device_id_type=MESH,
        )


    def half_copy(hop):
        if hop == 0:
            src, dst, to = a_all.at[z, yh, x], normal.at[:, pl.ds(0, EDGE)], (across, col)
        else:
            src, dst, to = normal.at[:, pl.ds(0, EDGE)], a_all.at[z, yh, x], (across, col_at(0, 0, PARTNER))
        return pltpu.make_async_remote_copy(
            src_ref=src, dst_ref=dst, send_sem=h_send.at[hop], recv_sem=h_recv.at[hop], device_id=to, device_id_type=MESH
        )

    def half_arrival():
        dst = a_all.at[z, 1 - yh, x]
        return pltpu.make_async_remote_copy(
            src_ref=dst, dst_ref=dst, send_sem=h_send.at[1], recv_sem=h_recv.at[1],
            device_id=(across, col_at(0, 0, PARTNER)), device_id_type=MESH,
        )

    def b_slab(py, pc, chunk):
        first, count = CHUNKS[chunk]
        return b_all.at[py * 2 + pc, pl.ds(first, count), :]

    def b_copy(sign, d, chunk, py):
        way = 0 if sign > 0 else 1
        return pltpu.make_async_remote_copy(
            src_ref=b_slab(py, core, chunk), dst_ref=b_slab(py, core, chunk),
            send_sem=b_send.at[way, d, chunk], recv_sem=b_recv.at[way, d, chunk],
            device_id=((y + sign) * 2 + core, col), device_id_type=MESH,
        )

    def sends(sign, d):
        return (y >= d) & (y <= 2) if sign > 0 else (y + d <= 3) & (y >= 1)

    def receives(sign, d):
        return y >= 1 + d if sign > 0 else y + 1 + d <= 3

    def relays(sign, d):
        return receives(sign, d) & (y <= 2 if sign > 0 else y >= 1)

    def ends(sign, d):
        return receives(sign, d) & (y == 3 if sign > 0 else y == 0)

    def sibling_copy(kind, chunk, py, pc):
        return pltpu.make_async_remote_copy(
            src_ref=b_slab(py, pc, chunk), dst_ref=b_slab(py, pc, chunk),
            send_sem=s_send.at[kind, chunk], recv_sem=s_recv.at[kind, chunk],
            device_id=(y * 2 + 1 - core, col), device_id_type=MESH,
        )

    def kind_of(sign, d):
        return 1 + d if sign > 0 else 4 + d

    def b_own(sign, chunk):
        @pl.when(sends(sign, 0))
        def _():
            b_copy(sign, 0, chunk, y).start()

    def b_arrival(sign, d, chunk, forward):
        @pl.when(relays(sign, d) if forward else ends(sign, d))
        def _():
            py = y - sign * (1 + d)
            b_copy(sign, d, chunk, py).wait_recv()
            if forward:
                b_copy(sign, d + 1, chunk, py).start()
            sibling_copy(kind_of(sign, d), chunk, py, core).start()

    half_copy(0).start()
    for k, m in enumerate(msgs):
        if m["out"] == (0, OWN, 0, "full"):
            a_copy(k, m["out"]).start()
    for sign in (1, -1):
        b_own(sign, 0)
    half_copy(0).wait_recv()
    half_copy(1).start()
    for sign in (1, -1):
        b_own(sign, 1)
    for chunk in range(2):
        sibling_copy(0, chunk, y, core).start()

    bands = [band_ref[0, 0, t, 0] for t in range(12)]
    places = []
    for t in range(12):
        rank = jnp.int32(0)
        for u in range(t):
            rank = rank + jnp.where(bands[u] == bands[t], 1, 0)
        places.append(bands[t] * 2 + rank)
    for p in range(16):
        which, any_of = jnp.int32(0), jnp.int32(0)
        for t in range(12):
            hit = places[t] == p
            which = jnp.where(hit, t, which)
            any_of = jnp.where(hit, 1, any_of)
        slot_of[p] = which
        filled[p] = any_of

    extra = []
    for d in range(2):
        for chunk, late in ((0, 12.5), (1, 25.5)):
            for sign in (1, -1):
                extra.append((17.0 * d + late, functools.partial(b_arrival, sign, d, chunk, True)))
    for d, late in ((0, 33.0), (1, 46.0)):
        for chunk in range(2):
            for sign in (1, -1):
                extra.append((late, functools.partial(b_arrival, sign, d, chunk, False)))
    extra.sort(key=lambda e: e[0])
    for t, what, k in steps:
        while extra and extra[0][0] <= t:
            extra.pop(0)[1]()
        if what == "wait":
            a_copy(k, msgs[k]["in"]).wait_recv()
        elif what == "partner":
            half_arrival().wait_recv()
        elif msgs[k]["out"] != (0, OWN, 0, "full"):
            a_copy(k, msgs[k]["out"]).start()
    for _, act in extra:
        act()

    def sibling_arrived(kind, py):
        for chunk in range(2):
            sibling_copy(kind, chunk, py, 1 - core).wait_recv()

    sibling_arrived(0, y)
    for d in range(2):
        for sign in (1, -1):
            @pl.when(receives(sign, d))
            def _():
                sibling_arrived(kind_of(sign, d), y - sign * (1 + d))

    def multiply(i):
        near = i // 2
        py = jnp.where(y < 2, near, 3 - near)
        slab = py * 2 + i % 2
        left = jnp.concatenate([a_all[slab, h, k] for h in range(2) for k in range(4)], axis=1)
        return jnp.dot(left, b_all[slab], preferred_element_type=jnp.float32)

    acc[...] = jnp.zeros_like(acc)

    def more(i, carry):
        acc[...] += multiply(i)
        return carry

    lax.fori_loop(0, 6, more, 0)
    for chunk in range(2):
        for sign in (1, -1):
            b_arrival(sign, 2, chunk, False)
    for sign in (1, -1):
        @pl.when(receives(sign, 2))
        def _():
            sibling_arrived(kind_of(sign, 2), y - sign * 3)
    lax.fori_loop(6, 8, more, 0)

    for c in range(3):
        cols = pl.ds(c * EDGE, EDGE)
        total = jnp.zeros((1, EDGE), jnp.float32)
        for r in range(4):
            rows = pl.ds(r * EDGE, EDGE)
            tile = acc[rows, cols]
            tile = jnp.where(keep_ref[r, c] != 0, tile * tile, jnp.zeros_like(tile))
            acc[rows, cols] = tile
            total = total + jnp.sum(tile, axis=0, keepdims=True)
        sums[row, :, cols] = total

    def sum_copy(k, who):
        return pltpu.make_async_remote_copy(
            src_ref=sums.at[who], dst_ref=sums.at[who], send_sem=c_send.at[k], recv_sem=c_recv.at[k],
            device_id=(row_peer(k), col), device_id_type=MESH,
        )

    for k in range(7, 0, -1):
        sum_copy(k, row).start()
    for k in range(7, 0, -1):
        sum_copy(k, row_peer(k)).wait_recv()

    half_copy(1).wait_send()
    total = sums[0]
    for i in range(1, 8):
        total = total + sums[i]
    scale = 1.0 / (total / (8 * 512) + 1e-5)
    for r in range(4):
        for c in range(3):
            rows, cols = pl.ds(r * EDGE, EDGE), pl.ds(c * EDGE, EDGE)
            tile = (acc[rows, cols] * scale[:, c * EDGE:(c + 1) * EDGE]).astype(jnp.bfloat16)
            normal[rows, cols] = tile
            tiles[r * 3 + c] = tile

    for p in range(16):
        tile = tiles[slot_of[p]]
        outgoing[p // 2, p % 2] = jnp.where(filled[p] != 0, tile, jnp.zeros_like(tile))

    def move(k, who):
        return pltpu.make_async_remote_copy(
            src_ref=outgoing.at[row_peer(k)], dst_ref=moved_ref.at[who], send_sem=r_send.at[k], recv_sem=r_recv.at[k],
            device_id=(row_peer(k), col), device_id_type=MESH,
        )

    for k in range(7, 0, -1):
        move(k, row).start()
    keep = pltpu.make_async_copy(outgoing.at[row], moved_ref.at[row], local_sem.at[0])
    keep.start()
    result = pltpu.make_async_copy(normal, out_ref, local_sem.at[1])
    result.start()

    half_copy(0).wait_send()
    for k, m in enumerate(msgs):
        a_copy(k, m["out"]).wait_send()
    for d in range(3):
        for sign in (1, -1):
            @pl.when(sends(sign, d))
            def _():
                for chunk in range(2):
                    b_copy(sign, d, chunk, y - sign * d).wait_send()

            @pl.when(receives(sign, d))
            def _():
                for chunk in range(2):
                    sibling_copy(kind_of(sign, d), chunk, y - sign * (1 + d), core).wait_send()
    for chunk in range(2):
        sibling_copy(0, chunk, y, core).wait_send()
    for k in range(7, 0, -1):
        sum_copy(k, row).wait_send()
    keep.wait()
    result.wait()
    for k in range(7, 0, -1):
        move(k, row).wait_send()
        move(k, row_peer(k)).wait_recv()


def body(a, b, a_support, b_support, keep, bands):
    count = len(build_messages())
    dma = pltpu.SemaphoreType.DMA
    vmem, smem = pl.BlockSpec(memory_space=pltpu.VMEM), pl.BlockSpec(memory_space=pltpu.SMEM)
    anywhere = pl.BlockSpec(memory_space=pl.ANY)
    out, moved = pl.pallas_call(
        kernel,
        out_shape=(
            jax.ShapeDtypeStruct((512, 384), jnp.bfloat16),
            jax.ShapeDtypeStruct((8, 2, EDGE, EDGE), jnp.bfloat16),
        ),
        in_specs=[vmem, vmem, smem, smem, smem, smem],
        out_specs=(anywhere, anywhere),
        scratch_shapes=[
            pltpu.VMEM((8, 2, 4, 512, EDGE), jnp.bfloat16),
            pltpu.VMEM((8, 1024, 384), jnp.bfloat16),
            pltpu.VMEM((512, 384), jnp.float32),
            pltpu.VMEM((12, EDGE, EDGE), jnp.bfloat16),
            pltpu.VMEM((512, 384), jnp.bfloat16),
            pltpu.VMEM((8, 2, EDGE, EDGE), jnp.bfloat16),
            pltpu.VMEM((8, 1, 384), jnp.float32),
            pltpu.SMEM((16,), jnp.int32),
            pltpu.SMEM((16,), jnp.int32),
            dma((count,)), dma((count,)),
            dma((2, 3, 2)), dma((2, 3, 2)),
            dma((7, 2)), dma((7, 2)),
            dma((2,)), dma((2,)),
            dma((8,)), dma((8,)),
            dma((8,)), dma((8,)),
            dma((2,)),
        ],
        compiler_params=pltpu.CompilerParams(
            collective_id=0, has_side_effects=True, vmem_limit_bytes=40 * 1024 * 1024
        ),
        name="expand_and_move",
    )(a, b, a_support, b_support, keep, bands)
    return out, moved.reshape(2048, EDGE)


def solution(mesh):
    split = P("row", "col")
    return jax.shard_map(
        body,
        mesh=mesh,
        in_specs=(split, split, split, split, split, P("row", "col", None, None)),
        out_specs=(split, split),
        check_vma=False,
    )
```

```python
import functools
import heapq

import jax
import jax.numpy as jnp
from jax import lax
from jax.experimental import pallas as pl
from jax.experimental.pallas import tpu as pltpu
from jax.sharding import PartitionSpec as P

MESH = pl.DeviceIdType.MESH
EDGE = 128
OWN, PARTNER = 0, 1
PARTS = {"full": (0, 512), "top": (0, 256), "bot": (256, 256)}
CHUNKS = ((0, 256), (256, 768))
PARTNER_READY = 12.0
BLOCK_US, HOP_US = 2.82, 1.8


def build_messages():
    msgs = []

    def add(axis, sign, dz, half, dx, part, level):
        came = (dz - sign, half, dx, part) if axis == "z" else (dz, half, dx - sign, part)
        msgs.append({"axis": axis, "sign": sign, "out": (dz, half, dx, part), "in": came, "level": level})

    for sign in (1, -1):
        add("x", sign, 0, OWN, 0, "full", 0)
    for sign in (1, -1):
        add("x", sign, 0, OWN, -sign, "top" if sign > 0 else "bot", 0)
    for dx in (0, -1, 1, 2):
        for step in range(4):
            for sign in (1, -1):
                part = "full" if step < 3 else ("top" if sign > 0 else "bot")
                add("z", sign, -sign * step, OWN, dx, part, 2 + step)
    for step in range(4):
        for sign in (1, -1):
            part = "full" if step < 3 else ("top" if sign > 0 else "bot")
            add("z", sign, -sign * step, PARTNER, 0, part, 1)
    for dz in (0, -1, 1, -2, 2, -3, 3, 4):
        for sign in (1, -1):
            add("x", sign, dz, PARTNER, 0, "full", 1)
        for sign in (1, -1):
            add("x", sign, dz, PARTNER, -sign, "top" if sign > 0 else "bot", 1)
    return msgs


def halves(block):
    dz, half, dx, part = block
    key = (dz % 8, half, dx % 4)
    return {key + ("top",), key + ("bot",)} if part == "full" else {key + (part,)}


def plan(msgs):
    source = {}
    for k, m in enumerate(msgs):
        for h in halves(m["in"]):
            source[h] = k
    needs = [{source[h] for h in halves(m["out"]) if h in source} for m in msgs]
    left = [set(n) for n in needs]
    links = [("x", 1), ("x", -1), ("z", 1), ("z", -1)]
    busy = {link: 0.0 for link in links}
    waiting = {link: [] for link in links}
    issued = {link: 0.0 for link in links}
    ready, arrived, starts = {}, {}, []
    events = []
    for k, m in enumerate(msgs):
        if not needs[k]:
            heapq.heappush(events, (PARTNER_READY if m["out"][1] == PARTNER else 0.0, 0, k))
    while events:
        t, kind, k = heapq.heappop(events)
        touched = links
        if kind == 0:
            m = msgs[k]
            ready[k] = t
            touched = [(m["axis"], m["sign"])]
            heapq.heappush(waiting[touched[0]], (m["level"], k))
        elif kind == 2:
            for n, rest in enumerate(left):
                if k in rest:
                    rest.discard(k)
                    if not rest:
                        heapq.heappush(events, (t, 0, n))
        for link in touched:
            if busy[link] <= t and waiting[link]:
                n = heapq.heappop(waiting[link])[1]
                busy[link] = t + PARTS[msgs[n]["out"][3]][1] / 512 * BLOCK_US
                arrived[n] = busy[link] + HOP_US
                issued[link] = max(issued[link], ready[n])
                starts.append((issued[link], n))
                heapq.heappush(events, (busy[link], 1, n))
                heapq.heappush(events, (arrived[n], 2, n))
    starts.sort(key=lambda e: e[0])
    relayed = set().union(*needs)
    waited = set()
    steps = []
    for t, k in starts:
        for n in sorted(needs[k], key=lambda i: arrived[i]):
            if n not in waited:
                waited.add(n)
                steps.append((t, "wait", n))
        if msgs[k]["out"][1] == PARTNER and "partner" not in waited:
            waited.add("partner")
            steps.append((t, "partner", 0))
        steps.append((t, "start", k))
    groups = {}
    for k, m in enumerate(msgs):
        if k not in relayed:
            groups.setdefault((m["in"][0] % 8, m["in"][1]), []).append(k)
    for g, members in groups.items():
        steps.append((max(arrived[k] for k in members), "group", g))
    steps.sort(key=lambda e: e[0])
    return steps, sorted(groups), relayed


def kernel(
    a_hbm, b_hbm, asup_hbm, bsup_hbm, keep_hbm, band_hbm,
    out_ref, moved_ref,
    a_all, b_all, acc, tiles, outgoing, sums, relay, a_in, b_in,
    asup_ref, bsup_ref, keep_ref, band_ref, slot_of, filled,
    a_send, a_recv, g_recv, b_send, b_recv, s_send, s_recv, h_recv, c_send, c_recv, r_send, r_recv, local_sem,
):
    row, col = lax.axis_index("row"), lax.axis_index("col")
    y, core = row // 2, row % 2
    z, yh, x = col // 8, (col // 4) % 2, col % 4
    msgs = build_messages()
    steps, groups, relayed = plan(msgs)

    def row_peer(k):
        py = (3 - y, (y + 2) % 4, y + 1 - 2 * (y % 2), y)[3 - k // 2]
        pc = 1 - core if k % 2 else core
        return py * 2 + pc

    def col_at(dz, dx, half):
        h = yh if half == OWN else 1 - yh
        return ((z + dz + 8) % 8) * 8 + h * 4 + (x + dx + 4) % 4

    across = ((y + 2) % 4) * 2 + core
    neighbours = [(row, col_at(0, 1, OWN)), (row, col_at(0, -1, OWN)), (row, col_at(1, 0, OWN)), (row, col_at(-1, 0, OWN))]
    neighbours += [(row_peer(k), col) for k in range(1, 8)]
    neighbours.append((across, col_at(0, 0, PARTNER)))

    barrier = pltpu.get_barrier_semaphore()
    for device in neighbours:
        pl.semaphore_signal(barrier, inc=1, device_id=device, device_id_type=MESH)

    loads = [
        pltpu.make_async_copy(src, dst, local_sem.at[k])
        for k, (src, dst) in enumerate(
            ((asup_hbm, asup_ref), (a_hbm, a_in), (bsup_hbm, bsup_ref), (b_hbm, b_in), (keep_hbm, keep_ref), (band_hbm, band_ref))
        )
    ]
    for load in loads:
        load.start()

    loads[0].wait()
    loads[1].wait()
    for r in range(4):
        rows = pl.ds(r * EDGE, EDGE)
        tile = a_in[rows, :]
        a_all[z, yh, x, rows, :] = jnp.where(asup_ref[0, r] != 0, tile, jnp.zeros_like(tile))

    pl.semaphore_wait(barrier, len(neighbours))

    def block(spec):
        dz, half, dx, part = spec
        first, count = PARTS[part]
        h = yh if half == OWN else 1 - yh
        return a_all.at[(z + dz + 8) % 8, h, (x + dx + 4) % 4, pl.ds(first, count), :]

    def a_copy(k, spec):
        m = msgs[k]
        to = col_at(m["sign"], 0, OWN) if m["axis"] == "z" else col_at(0, m["sign"], OWN)
        return pltpu.make_async_remote_copy(
            src_ref=block(spec), dst_ref=block(spec), send_sem=a_send.at[0], recv_sem=a_recv.at[k] if k in relayed else g_recv.at[groups.index((m["in"][0] % 8, m["in"][1]))],
            device_id=(row, to), device_id_type=MESH,
        )

    def group_arrived(g):
        dz, half = g
        ref = a_all.at[(z + dz) % 8, yh] if half == OWN else a_all.at[(z + dz) % 8, 1 - yh, (x + 2) % 4]
        pltpu.make_async_remote_copy(
            src_ref=ref, dst_ref=ref, send_sem=a_send.at[0], recv_sem=g_recv.at[groups.index(g)],
            device_id=(row, col_at(1, 0, OWN)), device_id_type=MESH,
        ).wait_recv()

    def half_copy(hop):
        if hop == 0:
            src, dst, to = a_all.at[z, yh, x], relay, (across, col)
        else:
            src, dst, to = relay, a_all.at[z, yh, x], (across, col_at(0, 0, PARTNER))
        return pltpu.make_async_remote_copy(
            src_ref=src, dst_ref=dst, send_sem=a_send.at[0], recv_sem=h_recv.at[hop], device_id=to, device_id_type=MESH
        )

    def half_arrival():
        dst = a_all.at[z, 1 - yh, x]
        return pltpu.make_async_remote_copy(
            src_ref=dst, dst_ref=dst, send_sem=a_send.at[0], recv_sem=h_recv.at[1],
            device_id=(across, col_at(0, 0, PARTNER)), device_id_type=MESH,
        )

    def b_slab(py, pc, chunk):
        first, count = CHUNKS[chunk]
        return b_all.at[py * 2 + pc, pl.ds(first, count), :]

    def b_copy(sign, d, chunk, py):
        way = 0 if sign > 0 else 1
        return pltpu.make_async_remote_copy(
            src_ref=b_slab(py, core, chunk), dst_ref=b_slab(py, core, chunk),
            send_sem=b_send.at[0], recv_sem=b_recv.at[way, d, chunk],
            device_id=((y + sign) * 2 + core, col), device_id_type=MESH,
        )

    def sends(sign, d):
        return (y >= d) & (y <= 2) if sign > 0 else (y + d <= 3) & (y >= 1)

    def receives(sign, d):
        return y >= 1 + d if sign > 0 else y + 1 + d <= 3

    def relays(sign, d):
        return receives(sign, d) & (y <= 2 if sign > 0 else y >= 1)

    def ends(sign, d):
        return receives(sign, d) & (y == 3 if sign > 0 else y == 0)

    def sibling_copy(kind, chunk, py, pc):
        return pltpu.make_async_remote_copy(
            src_ref=b_slab(py, pc, chunk), dst_ref=b_slab(py, pc, chunk),
            send_sem=s_send.at[0], recv_sem=s_recv.at[1 if kind in (3, 6) else 0],
            device_id=(y * 2 + 1 - core, col), device_id_type=MESH,
        )

    def kind_of(sign, d):
        return 1 + d if sign > 0 else 4 + d

    def b_own(sign, chunk):
        @pl.when(sends(sign, 0))
        def _():
            b_copy(sign, 0, chunk, y).start()

    def b_arrival(sign, d, chunk, forward):
        @pl.when(relays(sign, d) if forward else ends(sign, d))
        def _():
            py = y - sign * (1 + d)
            b_copy(sign, d, chunk, py).wait_recv()
            if forward:
                b_copy(sign, d + 1, chunk, py).start()
            sibling_copy(kind_of(sign, d), chunk, py, core).start()

    half_copy(0).start()
    for k, m in enumerate(msgs):
        if m["out"] == (0, OWN, 0, "full"):
            a_copy(k, m["out"]).start()
    loads[2].wait()
    loads[3].wait()
    for r in range(8):
        for c in range(3):
            rows, cols = pl.ds(r * EDGE, EDGE), pl.ds(c * EDGE, EDGE)
            tile = b_in[rows, cols]
            b_all[row, rows, cols] = jnp.where(bsup_ref[c, r] != 0, tile, jnp.zeros_like(tile))
    for sign in (1, -1):
        b_own(sign, 0)
    half_copy(0).wait_recv()
    half_copy(1).start()
    for sign in (1, -1):
        b_own(sign, 1)
    for chunk in range(2):
        sibling_copy(0, chunk, y, core).start()
    loads[4].wait()
    loads[5].wait()

    bands = [band_ref[0, t] for t in range(12)]
    places = []
    for t in range(12):
        rank = jnp.int32(0)
        for u in range(t):
            rank = rank + jnp.where(bands[u] == bands[t], 1, 0)
        places.append(bands[t] * 2 + rank)
    for p in range(16):
        which, any_of = jnp.int32(0), jnp.int32(0)
        for t in range(12):
            hit = places[t] == p
            which = jnp.where(hit, t, which)
            any_of = jnp.where(hit, 1, any_of)
        slot_of[p] = which
        filled[p] = any_of

    far = jnp.where(y == 0, 3, jnp.where(y == 3, 0, -1))

    def multiply(slab):
        left = jnp.concatenate([a_all[slab, h, k] for h in range(2) for k in range(4)], axis=1)
        acc[...] += jnp.dot(left, b_all[slab], preferred_element_type=jnp.float32)

    def early(dz):
        slab = (z + dz + 8) % 8

        @pl.when(slab // 2 != far)
        def _():
            multiply(slab)

    def siblings_arrived(count, late):
        ref = b_all.at[pl.ds(0, count)]
        pltpu.make_async_remote_copy(
            src_ref=ref, dst_ref=ref, send_sem=s_send.at[0], recv_sem=s_recv.at[late],
            device_id=(y * 2 + 1 - core, col), device_id_type=MESH,
        ).wait_recv()

    def early_siblings():
        pl.when(far >= 0)(lambda: siblings_arrived(3, 0))
        pl.when(far < 0)(lambda: siblings_arrived(4, 0))

    acc[...] = jnp.zeros_like(acc)

    extra = []
    for d in range(2):
        for chunk, late in ((0, 12.5), (1, 25.5)):
            for sign in (1, -1):
                extra.append((17.0 * d + late, functools.partial(b_arrival, sign, d, chunk, True)))
    for d, late in ((0, 33.0), (1, 43.5)):
        for chunk in range(2):
            for sign in (1, -1):
                extra.append((late, functools.partial(b_arrival, sign, d, chunk, False)))
    extra.append((45.5, early_siblings))
    for late, dz in ((46.0, 0), (47.0, -1), (48.0, 1), (49.0, -2), (50.0, 2), (51.0, -3), (52.0, 3), (99.0, 4)):
        extra.append((late, functools.partial(early, dz)))
    extra.sort(key=lambda e: e[0])
    for t, what, k in steps:
        while extra and extra[0][0] <= t:
            extra.pop(0)[1]()
        if what == "wait":
            a_copy(k, msgs[k]["in"]).wait_recv()
        elif what == "group":
            group_arrived(k)
        elif what == "partner":
            half_arrival().wait_recv()
        elif msgs[k]["out"] != (0, OWN, 0, "full") or msgs[k]["axis"] == "z" and False:
            a_copy(k, msgs[k]["out"]).start()
    for _, act in extra:
        act()

    for chunk in range(2):
        for sign in (1, -1):
            b_arrival(sign, 2, chunk, False)

    @pl.when(far >= 0)
    def _():
        def more(i, carry):
            @pl.when(i == 1)
            def _():
                siblings_arrived(1, 1)

            multiply(far * 2 + (core + i) % 2)
            return carry

        lax.fori_loop(0, 2, more, 0)

    for c in range(3):
        cols = pl.ds(c * EDGE, EDGE)
        total = jnp.zeros((1, EDGE), jnp.float32)
        for r in range(4):
            rows = pl.ds(r * EDGE, EDGE)
            tile = acc[rows, cols]
            tile = jnp.where(keep_ref[r, c] != 0, tile * tile, jnp.zeros_like(tile))
            acc[rows, cols] = tile
            total = total + jnp.sum(tile, axis=0, keepdims=True)
        sums[row, :, cols] = total

    def sum_copy(k, who):
        return pltpu.make_async_remote_copy(
            src_ref=sums.at[who], dst_ref=sums.at[who], send_sem=c_send.at[0], recv_sem=c_recv.at[0],
            device_id=(row_peer(k), col), device_id_type=MESH,
        )

    for k in range(7, 0, -1):
        sum_copy(k, row).start()
    all_sums = pltpu.make_async_remote_copy(
        src_ref=sums.at[pl.ds(0, 7)], dst_ref=sums.at[pl.ds(0, 7)], send_sem=c_send.at[0], recv_sem=c_recv.at[0],
        device_id=(row_peer(1), col), device_id_type=MESH,
    )
    all_sums.wait_recv()

    total = sums[0]
    for i in range(1, 8):
        total = total + sums[i]
    scale = 1.0 / (total / (8 * 512) + 1e-5)
    for r in range(4):
        for c in range(3):
            rows, cols = pl.ds(r * EDGE, EDGE), pl.ds(c * EDGE, EDGE)
            tile = (acc[rows, cols] * scale[:, c * EDGE:(c + 1) * EDGE]).astype(jnp.bfloat16)
            out_ref[rows, cols] = tile
            tiles[r * 3 + c] = tile

    for p in range(16):
        tile = tiles[slot_of[p]]
        outgoing[p // 2, p % 2] = jnp.where(filled[p] != 0, tile, jnp.zeros_like(tile))

    def move(k, who):
        return pltpu.make_async_remote_copy(
            src_ref=outgoing.at[row_peer(k)], dst_ref=moved_ref.at[who], send_sem=r_send.at[0], recv_sem=r_recv.at[0],
            device_id=(row_peer(k), col), device_id_type=MESH,
        )

    for k in range(7, 0, -1):
        move(k, row).start()
    moved_ref[row] = outgoing[row]

    def sent(ref, sem):
        pltpu.make_async_remote_copy(
            src_ref=ref, dst_ref=ref, send_sem=sem.at[0], recv_sem=r_recv.at[0], device_id=(row_peer(1), col), device_id_type=MESH
        ).wait_send()

    sent(a_all, a_send)
    pl.when(far >= 0)(lambda: sent(b_all.at[pl.ds(0, 1)], b_send))
    pl.when(far < 0)(lambda: sent(b_all.at[pl.ds(0, 5)], b_send))
    sent(b_all.at[pl.ds(0, 4)], s_send)
    all_sums.wait_send()
    every = pltpu.make_async_remote_copy(
        src_ref=outgoing.at[pl.ds(0, 7)], dst_ref=moved_ref.at[pl.ds(0, 7)], send_sem=r_send.at[0], recv_sem=r_recv.at[0],
        device_id=(row_peer(1), col), device_id_type=MESH,
    )
    every.wait_send()
    every.wait_recv()


def body(a, b, a_support, b_support, keep, bands):
    count = len(build_messages())
    dma = pltpu.SemaphoreType.DMA
    there = pl.BlockSpec(memory_space=pltpu.HBM)
    vmem = pl.BlockSpec(memory_space=pltpu.VMEM)
    out, moved = pl.pallas_call(
        kernel,
        out_shape=(
            jax.ShapeDtypeStruct((512, 384), jnp.bfloat16),
            jax.ShapeDtypeStruct((8, 2, EDGE, EDGE), jnp.bfloat16),
        ),
        in_specs=[there] * 6,
        out_specs=(vmem, vmem),
        scratch_shapes=[
            pltpu.VMEM((8, 2, 4, 512, EDGE), jnp.bfloat16),
            pltpu.VMEM((8, 1024, 384), jnp.bfloat16),
            pltpu.VMEM((512, 384), jnp.float32),
            pltpu.VMEM((12, EDGE, EDGE), jnp.bfloat16),
            pltpu.VMEM((8, 2, EDGE, EDGE), jnp.bfloat16),
            pltpu.VMEM((8, 1, 384), jnp.float32),
            pltpu.VMEM((512, EDGE), jnp.bfloat16),
            pltpu.VMEM((512, EDGE), jnp.bfloat16),
            pltpu.VMEM((1024, 384), jnp.bfloat16),
            pltpu.SMEM((1, 4), jnp.int32),
            pltpu.SMEM((3, 8), jnp.int32),
            pltpu.SMEM((4, 3), jnp.int32),
            pltpu.SMEM((1, 12), jnp.int32),
            pltpu.SMEM((16,), jnp.int32),
            pltpu.SMEM((16,), jnp.int32),
            dma((1,)), dma((count,)), dma((9,)),
            dma((1,)), dma((2, 3, 2)),
            dma((1,)), dma((2,)),
            dma((2,)),
            dma((1,)), dma((1,)),
            dma((1,)), dma((1,)),
            dma((6,)),
        ],
        compiler_params=pltpu.CompilerParams(
            collective_id=0, has_side_effects=True, vmem_limit_bytes=67043328
        ),
        name="expand_and_move",
    )(a, b, a_support.T, b_support.T, keep, bands.reshape(1, 12))
    return out, moved.reshape(2048, EDGE)


def solution(mesh):
    split = P("row", "col")
    return jax.shard_map(
        body,
        mesh=mesh,
        in_specs=(split, split, split, split, split, P("row", "col", None, None)),
        out_specs=(split, split),
        check_vma=False,
    )
```

```python
import functools
import heapq

import jax
import jax.numpy as jnp
from jax import lax
from jax.experimental import pallas as pl
from jax.experimental.pallas import tpu as pltpu
from jax.sharding import PartitionSpec as P

MESH = pl.DeviceIdType.MESH
EDGE = 128
OWN, PARTNER = 0, 1
PARTS = {"full": (0, 512), "top": (0, 256), "bot": (256, 256)}
CHUNKS = ((0, 256), (256, 256), (512, 256), (768, 256))
BY_Z = ((1,), (1, 2))
PARTNER_READY = 12.0
BLOCK_US, HOP_US = 2.82, 1.8


def build_messages():
    msgs = []

    def add(axis, sign, dz, half, dx, part, level):
        came = (dz - sign, half, dx, part) if axis == "z" else (dz, half, dx - sign, part)
        msgs.append({"axis": axis, "sign": sign, "out": (dz, half, dx, part), "in": came, "level": level})

    for half in (OWN, PARTNER):
        for dx in (0, -1, 1, 2):
            for step in range(4):
                for sign in (1, -1):
                    if dx == 0 or step + 1 in BY_Z[half]:
                        part = "full" if step < 3 else ("top" if sign > 0 else "bot")
                        level = (0 if dx == 0 else 2) + step * 0.1
                        add("z", sign, -sign * step, half, dx, part, level)
        for dz in (0, -1, 1, -2, 2, -3, 3, 4):
            if abs(dz) not in BY_Z[half]:
                for sign in (1, -1):
                    add("x", sign, dz, half, 0, "full", abs(dz) * 0.1 + 0.5)
                for sign in (1, -1):
                    add("x", sign, dz, half, -sign, "top" if sign > 0 else "bot", abs(dz) * 0.1)
    return msgs


def halves(block):
    dz, half, dx, part = block
    key = (dz % 8, half, dx % 4)
    return {key + ("top",), key + ("bot",)} if part == "full" else {key + (part,)}


def group_of(m):
    return m["in"][0] % 8, m["in"][1]


def plan(msgs):
    source = {}
    for k, m in enumerate(msgs):
        for h in halves(m["in"]):
            source[h] = k
    needs = [{source[h] for h in halves(m["out"]) if h in source} for m in msgs]
    left = [set(n) for n in needs]
    links = [("x", 1), ("x", -1), ("z", 1), ("z", -1)]
    busy = {link: 0.0 for link in links}
    waiting = {link: [] for link in links}
    issued = {link: 0.0 for link in links}
    ready, arrived, starts = {}, {}, []
    events = []
    for k, m in enumerate(msgs):
        if not needs[k]:
            heapq.heappush(events, (PARTNER_READY if m["out"][1] == PARTNER else 0.0, 0, k))
    while events:
        t, kind, k = heapq.heappop(events)
        touched = links
        if kind == 0:
            m = msgs[k]
            ready[k] = t
            touched = [(m["axis"], m["sign"])]
            heapq.heappush(waiting[touched[0]], (m["level"], k))
        elif kind == 2:
            for n, rest in enumerate(left):
                if k in rest:
                    rest.discard(k)
                    if not rest:
                        heapq.heappush(events, (t, 0, n))
        for link in touched:
            if busy[link] <= t and waiting[link]:
                n = heapq.heappop(waiting[link])[1]
                busy[link] = t + PARTS[msgs[n]["out"][3]][1] / 512 * BLOCK_US
                arrived[n] = busy[link] + HOP_US
                issued[link] = max(issued[link], ready[n])
                starts.append((issued[link], n))
                heapq.heappush(events, (busy[link], 1, n))
                heapq.heappush(events, (arrived[n], 2, n))
    starts.sort(key=lambda e: e[0])
    relayed = set().union(*needs)
    waited = set()
    steps = []
    for t, k in starts:
        for n in sorted(needs[k], key=lambda i: arrived[i]):
            if n not in waited:
                waited.add(n)
                steps.append((t, "wait", n))
        if msgs[k]["out"][1] == PARTNER and "partner" not in waited:
            waited.add("partner")
            steps.append((t, "partner", 0))
        steps.append((t, "start", k))
    groups = {}
    for k, m in enumerate(msgs):
        if k not in relayed:
            groups.setdefault(group_of(m), []).append(k)
    for g, members in groups.items():
        steps.append((max(arrived[k] for k in members), "group", g))
    steps.sort(key=lambda e: e[0])
    return steps, sorted(groups), relayed


def kernel(
    a_hbm, b_hbm, asup_hbm, bsup_hbm, keep_hbm, band_hbm,
    out_ref, moved_ref,
    a_all, b_all, acc, tiles, outgoing, sums, relay, a_in, b_in,
    asup_ref, bsup_ref, keep_ref, band_ref, slot_of, filled,
    a_send, a_recv, g_recv, b_send, b_recv, s_send, s_recv, h_recv, c_send, c_recv, r_send, r_recv, local_sem,
):
    row, col = lax.axis_index("row"), lax.axis_index("col")
    y, core = row // 2, row % 2
    z, yh, x = col // 8, (col // 4) % 2, col % 4
    msgs = build_messages()
    steps, groups, relayed = plan(msgs)

    def row_peer(k):
        py = (3 - y, (y + 2) % 4, y + 1 - 2 * (y % 2), y)[3 - k // 2]
        pc = 1 - core if k % 2 else core
        return py * 2 + pc

    def col_at(dz, dx, half):
        h = yh if half == OWN else 1 - yh
        return ((z + dz + 8) % 8) * 8 + h * 4 + (x + dx + 4) % 4

    across = ((y + 2) % 4) * 2 + core
    neighbours = [(row, col_at(0, 1, OWN)), (row, col_at(0, -1, OWN)), (row, col_at(1, 0, OWN)), (row, col_at(-1, 0, OWN))]
    neighbours += [(row_peer(k), col) for k in range(1, 8)]
    neighbours.append((across, col_at(0, 0, PARTNER)))

    barrier = pltpu.get_barrier_semaphore()
    for device in neighbours:
        pl.semaphore_signal(barrier, inc=1, device_id=device, device_id_type=MESH)

    loads = [
        pltpu.make_async_copy(src, dst, local_sem.at[k])
        for k, (src, dst) in enumerate(
            ((asup_hbm, asup_ref), (a_hbm, a_in), (bsup_hbm, bsup_ref), (b_hbm, b_in), (keep_hbm, keep_ref), (band_hbm, band_ref))
        )
    ]
    for load in loads:
        load.start()

    loads[0].wait()
    loads[1].wait()
    for r in range(4):
        rows = pl.ds(r * EDGE, EDGE)
        tile = a_in[rows, :]
        a_all[z, yh, x, rows, :] = jnp.where(asup_ref[0, r] != 0, tile, jnp.zeros_like(tile))

    pl.semaphore_wait(barrier, len(neighbours))

    def block(spec):
        dz, half, dx, part = spec
        first, count = PARTS[part]
        h = yh if half == OWN else 1 - yh
        return a_all.at[(z + dz + 8) % 8, h, (x + dx + 4) % 4, pl.ds(first, count), :]

    def a_copy(k, spec):
        m = msgs[k]
        to = col_at(m["sign"], 0, OWN) if m["axis"] == "z" else col_at(0, m["sign"], OWN)
        return pltpu.make_async_remote_copy(
            src_ref=block(spec), dst_ref=block(spec), send_sem=a_send.at[0], recv_sem=a_recv.at[k] if k in relayed else g_recv.at[groups.index(group_of(m))],
            device_id=(row, to), device_id_type=MESH,
        )

    def group_arrived(g):
        dz, half = g
        size = sum(1 if m["in"][3] == "full" else 0.5 for k, m in enumerate(msgs) if k not in relayed and group_of(m) == g)
        ref = a_all.at[(z + dz) % 8, yh if half == OWN else 1 - yh, pl.ds(0, int(size))]
        pltpu.make_async_remote_copy(
            src_ref=ref, dst_ref=ref, send_sem=a_send.at[0], recv_sem=g_recv.at[groups.index(g)],
            device_id=(row, col_at(1, 0, OWN)), device_id_type=MESH,
        ).wait_recv()

    def half_copy(hop):
        if hop == 0:
            src, dst, to = a_all.at[z, yh, x], relay, (across, col)
        else:
            src, dst, to = relay, a_all.at[z, yh, x], (across, col_at(0, 0, PARTNER))
        return pltpu.make_async_remote_copy(
            src_ref=src, dst_ref=dst, send_sem=a_send.at[0], recv_sem=h_recv.at[hop], device_id=to, device_id_type=MESH
        )

    def half_arrival():
        dst = a_all.at[z, 1 - yh, x]
        return pltpu.make_async_remote_copy(
            src_ref=dst, dst_ref=dst, send_sem=a_send.at[0], recv_sem=h_recv.at[1],
            device_id=(across, col_at(0, 0, PARTNER)), device_id_type=MESH,
        )

    def b_slab(py, pc, chunk):
        first, count = CHUNKS[chunk]
        return b_all.at[py * 2 + pc, pl.ds(first, count), :]

    def b_copy(sign, d, chunk, py):
        way = 0 if sign > 0 else 1
        return pltpu.make_async_remote_copy(
            src_ref=b_slab(py, core, chunk), dst_ref=b_slab(py, core, chunk),
            send_sem=b_send.at[0], recv_sem=b_recv.at[way, d, chunk],
            device_id=((y + sign) * 2 + core, col), device_id_type=MESH,
        )

    def sends(sign, d):
        return (y >= d) & (y <= 2) if sign > 0 else (y + d <= 3) & (y >= 1)

    def receives(sign, d):
        return y >= 1 + d if sign > 0 else y + 1 + d <= 3

    def relays(sign, d):
        return receives(sign, d) & (y <= 2 if sign > 0 else y >= 1)

    def ends(sign, d):
        return receives(sign, d) & (y == 3 if sign > 0 else y == 0)

    def sibling_copy(kind, chunk, py, pc):
        return pltpu.make_async_remote_copy(
            src_ref=b_slab(py, pc, chunk), dst_ref=b_slab(py, pc, chunk),
            send_sem=s_send.at[0], recv_sem=s_recv.at[(2 if chunk == 3 else 1) if kind in (3, 6) else 0],
            device_id=(y * 2 + 1 - core, col), device_id_type=MESH,
        )

    def kind_of(sign, d):
        return 1 + d if sign > 0 else 4 + d

    def b_own(sign, chunk):
        @pl.when(sends(sign, 0))
        def _():
            b_copy(sign, 0, chunk, y).start()

    def b_arrival(sign, d, chunk, forward):
        @pl.when(relays(sign, d) if forward else ends(sign, d))
        def _():
            py = y - sign * (1 + d)
            b_copy(sign, d, chunk, py).wait_recv()
            if forward:
                b_copy(sign, d + 1, chunk, py).start()
            sibling_copy(kind_of(sign, d), chunk, py, core).start()

    half_copy(0).start()
    for k, m in enumerate(msgs):
        if m["out"] == (0, OWN, 0, "full"):
            a_copy(k, m["out"]).start()
    loads[2].wait()
    loads[3].wait()
    for r in range(8):
        for c in range(3):
            rows, cols = pl.ds(r * EDGE, EDGE), pl.ds(c * EDGE, EDGE)
            tile = b_in[rows, cols]
            b_all[row, rows, cols] = jnp.where(bsup_ref[c, r] != 0, tile, jnp.zeros_like(tile))
    for sign in (1, -1):
        b_own(sign, 0)
    half_copy(0).wait_recv()
    half_copy(1).start()
    for chunk in range(1, 4):
        for sign in (1, -1):
            b_own(sign, chunk)
    for chunk in range(4):
        sibling_copy(0, chunk, y, core).start()
    loads[4].wait()
    loads[5].wait()

    bands = [band_ref[0, t] for t in range(12)]
    places = []
    for t in range(12):
        rank = jnp.int32(0)
        for u in range(t):
            rank = rank + jnp.where(bands[u] == bands[t], 1, 0)
        places.append(bands[t] * 2 + rank)
    for p in range(16):
        which, any_of = jnp.int32(0), jnp.int32(0)
        for t in range(12):
            hit = places[t] == p
            which = jnp.where(hit, t, which)
            any_of = jnp.where(hit, 1, any_of)
        slot_of[p] = which
        filled[p] = any_of

    far = jnp.where(y == 0, 3, jnp.where(y == 3, 0, -1))

    def multiply(slab, first=0, count=8):
        left = jnp.concatenate([a_all[slab, k // 4, k % 4] for k in range(first, first + count)], axis=1)
        right = b_all[slab, pl.ds(first * EDGE, count * EDGE), :]
        acc[...] += jnp.dot(left, right, preferred_element_type=jnp.float32)

    def early(dz):
        slab = (z + dz + 8) % 8

        @pl.when(slab // 2 != far)
        def _():
            multiply(slab)

    def siblings_arrived(ref, group):
        pltpu.make_async_remote_copy(
            src_ref=ref, dst_ref=ref, send_sem=s_send.at[0], recv_sem=s_recv.at[group],
            device_id=(y * 2 + 1 - core, col), device_id_type=MESH,
        ).wait_recv()

    def early_siblings():
        pl.when(far >= 0)(lambda: siblings_arrived(b_all.at[pl.ds(0, 3)], 0))
        pl.when(far < 0)(lambda: siblings_arrived(b_all.at[pl.ds(0, 4)], 0))

    acc[...] = jnp.zeros_like(acc)

    extra = []
    for d in range(2):
        for chunk in range(4):
            for sign in (1, -1):
                extra.append((17.0 * d + 4.25 * chunk + 14.5, functools.partial(b_arrival, sign, d, chunk, True)))
    for d, late in ((0, 33.0), (1, 45.5)):
        for chunk in range(4):
            for sign in (1, -1):
                extra.append((late, functools.partial(b_arrival, sign, d, chunk, False)))
    extra.append((46.3, early_siblings))
    for late, dz in ((46.31, 0), (46.32, -1), (46.33, 1), (46.34, -3), (47.75, 3), (48.8, -2), (48.81, 2), (99.0, 4)):
        extra.append((late, functools.partial(early, dz)))
    extra.sort(key=lambda e: e[0])
    for t, what, k in steps:
        while extra and extra[0][0] <= t:
            extra.pop(0)[1]()
        if what == "wait":
            a_copy(k, msgs[k]["in"]).wait_recv()
        elif what == "group":
            group_arrived(k)
        elif what == "partner":
            half_arrival().wait_recv()
        elif msgs[k]["out"] != (0, OWN, 0, "full"):
            a_copy(k, msgs[k]["out"]).start()
    for _, act in extra:
        act()

    def far_slabs(first, count, group):
        def more(i, carry):
            pl.when(i == 1)(lambda: siblings_arrived(b_all.at[0, pl.ds(0, count * EDGE)], group))
            multiply(far * 2 + (core + i) % 2, first, count)
            return carry

        @pl.when(far >= 0)
        def _():
            lax.fori_loop(0, 2, more, 0)

    for chunk in range(4):
        for sign in (1, -1):
            b_arrival(sign, 2, chunk, False)
        if chunk == 2:
            far_slabs(0, 6, 1)
    far_slabs(6, 2, 2)

    for c in range(3):
        cols = pl.ds(c * EDGE, EDGE)
        total = jnp.zeros((1, EDGE), jnp.float32)
        for r in range(4):
            rows = pl.ds(r * EDGE, EDGE)
            tile = acc[rows, cols]
            tile = jnp.where(keep_ref[r, c] != 0, tile * tile, jnp.zeros_like(tile))
            acc[rows, cols] = tile
            total = total + jnp.sum(tile, axis=0, keepdims=True)
        sums[row, :, cols] = total

    def sum_copy(k, who):
        return pltpu.make_async_remote_copy(
            src_ref=sums.at[who], dst_ref=sums.at[who], send_sem=c_send.at[0], recv_sem=c_recv.at[0],
            device_id=(row_peer(k), col), device_id_type=MESH,
        )

    for k in range(7, 0, -1):
        sum_copy(k, row).start()
    all_sums = pltpu.make_async_remote_copy(
        src_ref=sums.at[pl.ds(0, 7)], dst_ref=sums.at[pl.ds(0, 7)], send_sem=c_send.at[0], recv_sem=c_recv.at[0],
        device_id=(row_peer(1), col), device_id_type=MESH,
    )
    all_sums.wait_recv()

    total = sums[0]
    for i in range(1, 8):
        total = total + sums[i]
    scale = 1.0 / (total / (8 * 512) + 1e-5)
    for r in range(4):
        for c in range(3):
            rows, cols = pl.ds(r * EDGE, EDGE), pl.ds(c * EDGE, EDGE)
            tile = (acc[rows, cols] * scale[:, c * EDGE:(c + 1) * EDGE]).astype(jnp.bfloat16)
            out_ref[rows, cols] = tile
            tiles[r * 3 + c] = tile

    for p in range(16):
        tile = tiles[slot_of[p]]
        outgoing[p // 2, p % 2] = jnp.where(filled[p] != 0, tile, jnp.zeros_like(tile))

    def move(k, who):
        return pltpu.make_async_remote_copy(
            src_ref=outgoing.at[row_peer(k)], dst_ref=moved_ref.at[who], send_sem=r_send.at[0], recv_sem=r_recv.at[0],
            device_id=(row_peer(k), col), device_id_type=MESH,
        )

    for k in range(7, 0, -1):
        move(k, row).start()
    moved_ref[row] = outgoing[row]

    def sent(ref, sem):
        pltpu.make_async_remote_copy(
            src_ref=ref, dst_ref=ref, send_sem=sem.at[0], recv_sem=r_recv.at[0], device_id=(row_peer(1), col), device_id_type=MESH
        ).wait_send()

    sent(a_all, a_send)
    pl.when(far >= 0)(lambda: sent(b_all.at[pl.ds(0, 1)], b_send))
    pl.when(far < 0)(lambda: sent(b_all.at[pl.ds(0, 5)], b_send))
    sent(b_all.at[pl.ds(0, 4)], s_send)
    all_sums.wait_send()
    every = pltpu.make_async_remote_copy(
        src_ref=outgoing.at[pl.ds(0, 7)], dst_ref=moved_ref.at[pl.ds(0, 7)], send_sem=r_send.at[0], recv_sem=r_recv.at[0],
        device_id=(row_peer(1), col), device_id_type=MESH,
    )
    every.wait_send()
    every.wait_recv()


def body(a, b, a_support, b_support, keep, bands):
    count = len(build_messages())
    dma = pltpu.SemaphoreType.DMA
    there = pl.BlockSpec(memory_space=pltpu.HBM)
    vmem = pl.BlockSpec(memory_space=pltpu.VMEM)
    out, moved = pl.pallas_call(
        kernel,
        out_shape=(
            jax.ShapeDtypeStruct((512, 384), jnp.bfloat16),
            jax.ShapeDtypeStruct((8, 2, EDGE, EDGE), jnp.bfloat16),
        ),
        in_specs=[there] * 6,
        out_specs=(vmem, vmem),
        scratch_shapes=[
            pltpu.VMEM((8, 2, 4, 512, EDGE), jnp.bfloat16),
            pltpu.VMEM((8, 1024, 384), jnp.bfloat16),
            pltpu.VMEM((512, 384), jnp.float32),
            pltpu.VMEM((12, EDGE, EDGE), jnp.bfloat16),
            pltpu.VMEM((8, 2, EDGE, EDGE), jnp.bfloat16),
            pltpu.VMEM((8, 1, 384), jnp.float32),
            pltpu.VMEM((512, EDGE), jnp.bfloat16),
            pltpu.VMEM((512, EDGE), jnp.bfloat16),
            pltpu.VMEM((1024, 384), jnp.bfloat16),
            pltpu.SMEM((1, 4), jnp.int32),
            pltpu.SMEM((3, 8), jnp.int32),
            pltpu.SMEM((4, 3), jnp.int32),
            pltpu.SMEM((1, 12), jnp.int32),
            pltpu.SMEM((16,), jnp.int32),
            pltpu.SMEM((16,), jnp.int32),
            dma((1,)), dma((count,)), dma((16,)),
            dma((1,)), dma((2, 3, 4)),
            dma((1,)), dma((3,)),
            dma((2,)),
            dma((1,)), dma((1,)),
            dma((1,)), dma((1,)),
            dma((6,)),
        ],
        compiler_params=pltpu.CompilerParams(
            collective_id=0, has_side_effects=True, vmem_limit_bytes=40 * 1024 * 1024
        ),
        name="expand_and_move",
    )(*(pltpu.with_memory_space_constraint(v, pltpu.HBM) for v in (a, b, a_support.T, b_support.T, keep, bands.reshape(1, 12))))
    return out, moved.reshape(2048, EDGE)


def solution(mesh):
    split = P("row", "col")
    return jax.shard_map(
        body,
        mesh=mesh,
        in_specs=(split, split, split, split, split, P("row", "col", None, None)),
        out_specs=(split, split),
        check_vma=False,
    )
```

```python
import functools
import heapq

import jax
import jax.numpy as jnp
from jax import lax
from jax.experimental import pallas as pl
from jax.experimental.pallas import tpu as pltpu
from jax.sharding import PartitionSpec as P

MESH = pl.DeviceIdType.MESH
EDGE = 128
OWN, PARTNER = 0, 1
PARTS = {"full": (0, 512), "top": (0, 256), "bot": (256, 256)}
CHUNKS = ((0, 256), (256, 256), (512, 256), (768, 256))
BY_Z = ((1,), (1, 2))
PARTNER_READY = 12.0
BLOCK_US, HOP_US = 2.82, 1.8


def build_messages():
    msgs = []

    def add(axis, sign, dz, half, dx, part, level):
        came = (dz - sign, half, dx, part) if axis == "z" else (dz, half, dx - sign, part)
        msgs.append({"axis": axis, "sign": sign, "out": (dz, half, dx, part), "in": came, "level": level})

    for half in (OWN, PARTNER):
        for dx in (0, -1, 1, 2):
            for step in range(4):
                for sign in (1, -1):
                    if dx == 0 or step + 1 in BY_Z[half]:
                        part = "full" if step < 3 else ("top" if sign > 0 else "bot")
                        level = (0 if dx == 0 else 2) + step * 0.1
                        add("z", sign, -sign * step, half, dx, part, level)
        for dz in (0, -1, 1, -2, 2, -3, 3, 4):
            if abs(dz) not in BY_Z[half]:
                for sign in (1, -1):
                    add("x", sign, dz, half, 0, "full", abs(dz) * 0.1 + 0.5)
                for sign in (1, -1):
                    add("x", sign, dz, half, -sign, "top" if sign > 0 else "bot", abs(dz) * 0.1)
    return msgs


def halves(block):
    dz, half, dx, part = block
    key = (dz % 8, half, dx % 4)
    return {key + ("top",), key + ("bot",)} if part == "full" else {key + (part,)}


def group_of(m):
    return m["in"][0] % 8, m["in"][1]


def plan(msgs):
    source = {}
    for k, m in enumerate(msgs):
        for h in halves(m["in"]):
            source[h] = k
    needs = [{source[h] for h in halves(m["out"]) if h in source} for m in msgs]
    left = [set(n) for n in needs]
    links = [("x", 1), ("x", -1), ("z", 1), ("z", -1)]
    busy = {link: 0.0 for link in links}
    waiting = {link: [] for link in links}
    issued = {link: 0.0 for link in links}
    ready, arrived, starts = {}, {}, []
    events = []
    for k, m in enumerate(msgs):
        if not needs[k]:
            heapq.heappush(events, (PARTNER_READY if m["out"][1] == PARTNER else 0.0, 0, k))
    while events:
        t, kind, k = heapq.heappop(events)
        touched = links
        if kind == 0:
            m = msgs[k]
            ready[k] = t
            touched = [(m["axis"], m["sign"])]
            heapq.heappush(waiting[touched[0]], (m["level"], k))
        elif kind == 2:
            for n, rest in enumerate(left):
                if k in rest:
                    rest.discard(k)
                    if not rest:
                        heapq.heappush(events, (t, 0, n))
        for link in touched:
            if busy[link] <= t and waiting[link]:
                n = heapq.heappop(waiting[link])[1]
                busy[link] = t + PARTS[msgs[n]["out"][3]][1] / 512 * BLOCK_US
                arrived[n] = busy[link] + HOP_US
                issued[link] = max(issued[link], ready[n])
                starts.append((issued[link], n))
                heapq.heappush(events, (busy[link], 1, n))
                heapq.heappush(events, (arrived[n], 2, n))
    starts.sort(key=lambda e: e[0])
    relayed = set().union(*needs)
    waited = set()
    steps = []
    for t, k in starts:
        for n in sorted(needs[k], key=lambda i: arrived[i]):
            if n not in waited:
                waited.add(n)
                steps.append((t, "wait", n))
        if msgs[k]["out"][1] == PARTNER and "partner" not in waited:
            waited.add("partner")
            steps.append((t, "partner", 0))
        steps.append((t, "start", k))
    groups = {}
    for k, m in enumerate(msgs):
        if k not in relayed:
            groups.setdefault(group_of(m), []).append(k)
    for g, members in groups.items():
        steps.append((max(arrived[k] for k in members), "group", g))
    steps.sort(key=lambda e: e[0])
    return steps, sorted(groups), relayed


def kernel(
    a_hbm, b_hbm, asup_hbm, bsup_hbm, keep_hbm, band_hbm,
    out_ref, moved_ref,
    a_all, b_all, acc, tiles, slots, scales, outgoing, sums, relay, a_in, b_in,
    asup_ref, bsup_ref, keep_ref, band_ref, slot_of, filled, third_of,
    a_send, a_recv, g_recv, b_send, b_recv, s_send, s_recv, h_recv, c_send, c_recv, r_send, r_recv, local_sem,
):
    row, col = lax.axis_index("row"), lax.axis_index("col")
    y, core = row // 2, row % 2
    z, yh, x = col // 8, (col // 4) % 2, col % 4
    msgs = build_messages()
    steps, groups, relayed = plan(msgs)

    def row_peer(k):
        py = (3 - y, (y + 2) % 4, y + 1 - 2 * (y % 2), y)[3 - k // 2]
        pc = 1 - core if k % 2 else core
        return py * 2 + pc

    def col_at(dz, dx, half):
        h = yh if half == OWN else 1 - yh
        return ((z + dz + 8) % 8) * 8 + h * 4 + (x + dx + 4) % 4

    across = ((y + 2) % 4) * 2 + core
    neighbours = [(row, col_at(0, 1, OWN)), (row, col_at(0, -1, OWN)), (row, col_at(1, 0, OWN)), (row, col_at(-1, 0, OWN))]
    neighbours += [(row_peer(k), col) for k in range(1, 8)]
    neighbours.append((across, col_at(0, 0, PARTNER)))

    barrier = pltpu.get_barrier_semaphore()
    for device in neighbours:
        pl.semaphore_signal(barrier, inc=1, device_id=device, device_id_type=MESH)

    loads = [
        pltpu.make_async_copy(src, dst, local_sem.at[k])
        for k, (src, dst) in enumerate(
            ((asup_hbm, asup_ref), (a_hbm, a_in), (bsup_hbm, bsup_ref), (b_hbm, b_in), (keep_hbm, keep_ref), (band_hbm, band_ref))
        )
    ]
    for load in loads:
        load.start()

    loads[0].wait()
    loads[1].wait()
    for r in range(4):
        rows = pl.ds(r * EDGE, EDGE)
        tile = a_in[rows, :]
        a_all[z, yh, x, rows, :] = jnp.where(asup_ref[0, r] != 0, tile, jnp.zeros_like(tile))

    pl.semaphore_wait(barrier, len(neighbours))

    def block(spec):
        dz, half, dx, part = spec
        first, count = PARTS[part]
        h = yh if half == OWN else 1 - yh
        return a_all.at[(z + dz + 8) % 8, h, (x + dx + 4) % 4, pl.ds(first, count), :]

    def a_copy(k, spec):
        m = msgs[k]
        to = col_at(m["sign"], 0, OWN) if m["axis"] == "z" else col_at(0, m["sign"], OWN)
        return pltpu.make_async_remote_copy(
            src_ref=block(spec), dst_ref=block(spec), send_sem=a_send.at[0], recv_sem=a_recv.at[k] if k in relayed else g_recv.at[groups.index(group_of(m))],
            device_id=(row, to), device_id_type=MESH,
        )

    def group_arrived(g):
        dz, half = g
        size = sum(1 if m["in"][3] == "full" else 0.5 for k, m in enumerate(msgs) if k not in relayed and group_of(m) == g)
        ref = a_all.at[(z + dz) % 8, yh if half == OWN else 1 - yh, pl.ds(0, int(size))]
        pltpu.make_async_remote_copy(
            src_ref=ref, dst_ref=ref, send_sem=a_send.at[0], recv_sem=g_recv.at[groups.index(g)],
            device_id=(row, col_at(1, 0, OWN)), device_id_type=MESH,
        ).wait_recv()

    def half_copy(hop):
        if hop == 0:
            src, dst, to = a_all.at[z, yh, x], relay, (across, col)
        else:
            src, dst, to = relay, a_all.at[z, yh, x], (across, col_at(0, 0, PARTNER))
        return pltpu.make_async_remote_copy(
            src_ref=src, dst_ref=dst, send_sem=a_send.at[0], recv_sem=h_recv.at[hop], device_id=to, device_id_type=MESH
        )

    def half_arrival():
        dst = a_all.at[z, 1 - yh, x]
        return pltpu.make_async_remote_copy(
            src_ref=dst, dst_ref=dst, send_sem=a_send.at[0], recv_sem=h_recv.at[1],
            device_id=(across, col_at(0, 0, PARTNER)), device_id_type=MESH,
        )

    def b_slab(py, pc, chunk):
        first, count = CHUNKS[chunk]
        return b_all.at[py * 2 + pc, pl.ds(first, count), :]

    def b_copy(sign, d, chunk, py):
        way = 0 if sign > 0 else 1
        return pltpu.make_async_remote_copy(
            src_ref=b_slab(py, core, chunk), dst_ref=b_slab(py, core, chunk),
            send_sem=b_send.at[0], recv_sem=b_recv.at[way, d, chunk],
            device_id=((y + sign) * 2 + core, col), device_id_type=MESH,
        )

    def sends(sign, d):
        return (y >= d) & (y <= 2) if sign > 0 else (y + d <= 3) & (y >= 1)

    def receives(sign, d):
        return y >= 1 + d if sign > 0 else y + 1 + d <= 3

    def relays(sign, d):
        return receives(sign, d) & (y <= 2 if sign > 0 else y >= 1)

    def ends(sign, d):
        return receives(sign, d) & (y == 3 if sign > 0 else y == 0)

    def sibling_copy(kind, chunk, py, pc):
        return pltpu.make_async_remote_copy(
            src_ref=b_slab(py, pc, chunk), dst_ref=b_slab(py, pc, chunk),
            send_sem=s_send.at[0], recv_sem=s_recv.at[(2 if chunk == 3 else 1) if kind in (3, 6) else 0],
            device_id=(y * 2 + 1 - core, col), device_id_type=MESH,
        )

    def kind_of(sign, d):
        return 1 + d if sign > 0 else 4 + d

    def b_own(sign, chunk):
        @pl.when(sends(sign, 0))
        def _():
            b_copy(sign, 0, chunk, y).start()

    def b_arrival(sign, d, chunk, forward):
        @pl.when(relays(sign, d) if forward else ends(sign, d))
        def _():
            py = y - sign * (1 + d)
            b_copy(sign, d, chunk, py).wait_recv()
            if forward:
                b_copy(sign, d + 1, chunk, py).start()
            sibling_copy(kind_of(sign, d), chunk, py, core).start()

    half_copy(0).start()
    for k, m in enumerate(msgs):
        if m["out"] == (0, OWN, 0, "full"):
            a_copy(k, m["out"]).start()
    loads[2].wait()
    loads[3].wait()
    for r in range(8):
        for c in range(3):
            rows, cols = pl.ds(r * EDGE, EDGE), pl.ds(c * EDGE, EDGE)
            tile = b_in[rows, cols]
            b_all[row, rows, cols] = jnp.where(bsup_ref[c, r] != 0, tile, jnp.zeros_like(tile))
    for sign in (1, -1):
        b_own(sign, 0)
    half_copy(0).wait_recv()
    half_copy(1).start()
    for chunk in range(1, 4):
        for sign in (1, -1):
            b_own(sign, chunk)
    for chunk in range(4):
        sibling_copy(0, chunk, y, core).start()
    loads[4].wait()
    loads[5].wait()

    bands = [band_ref[0, t] for t in range(12)]
    places = []
    for t in range(12):
        rank = jnp.int32(0)
        for u in range(t):
            rank = rank + jnp.where(bands[u] == bands[t], 1, 0)
        places.append(bands[t] * 2 + rank)
    for p in range(16):
        which, any_of = jnp.int32(0), jnp.int32(0)
        for t in range(12):
            hit = places[t] == p
            which = jnp.where(hit, t, which)
            any_of = jnp.where(hit, 1, any_of)
        slot_of[p] = which
        third_of[p] = which % 3
        filled[p] = any_of

    far = jnp.where(y == 0, 3, jnp.where(y == 3, 0, -1))

    def multiply(slab, first=0, count=8):
        left = jnp.concatenate([a_all[slab, k // 4, k % 4] for k in range(first, first + count)], axis=1)
        right = b_all[slab, pl.ds(first * EDGE, count * EDGE), :]
        acc[...] += jnp.dot(left, right, preferred_element_type=jnp.float32)

    def early(dz):
        slab = (z + dz + 8) % 8

        @pl.when(slab // 2 != far)
        def _():
            multiply(slab)

    def siblings_arrived(ref, group):
        pltpu.make_async_remote_copy(
            src_ref=ref, dst_ref=ref, send_sem=s_send.at[0], recv_sem=s_recv.at[group],
            device_id=(y * 2 + 1 - core, col), device_id_type=MESH,
        ).wait_recv()

    def early_siblings():
        pl.when(far >= 0)(lambda: siblings_arrived(b_all.at[pl.ds(0, 3)], 0))
        pl.when(far < 0)(lambda: siblings_arrived(b_all.at[pl.ds(0, 4)], 0))

    acc[...] = jnp.zeros_like(acc)

    extra = []
    for d in range(2):
        for chunk in range(4):
            for sign in (1, -1):
                extra.append((17.0 * d + 4.25 * chunk + 14.5, functools.partial(b_arrival, sign, d, chunk, True)))
    for d, late in ((0, 33.0), (1, 45.5)):
        for chunk in range(4):
            for sign in (1, -1):
                extra.append((late, functools.partial(b_arrival, sign, d, chunk, False)))
    extra.append((46.3, early_siblings))
    for late, dz in ((46.31, 0), (46.32, -1), (46.33, 1), (46.34, -3), (47.75, 3), (48.8, -2), (48.81, 2), (99.0, 4)):
        extra.append((late, functools.partial(early, dz)))
    extra.sort(key=lambda e: e[0])
    for t, what, k in steps:
        while extra and extra[0][0] <= t:
            extra.pop(0)[1]()
        if what == "wait":
            a_copy(k, msgs[k]["in"]).wait_recv()
        elif what == "group":
            group_arrived(k)
        elif what == "partner":
            half_arrival().wait_recv()
        elif msgs[k]["out"] != (0, OWN, 0, "full"):
            a_copy(k, msgs[k]["out"]).start()
    for _, act in extra:
        act()

    def far_slabs(first, count, group):
        def more(i, carry):
            pl.when(i == 1)(lambda: siblings_arrived(b_all.at[0, pl.ds(0, count * EDGE)], group))
            multiply(far * 2 + (core + i) % 2, first, count)
            return carry

        @pl.when(far >= 0)
        def _():
            lax.fori_loop(0, 2, more, 0)

    for chunk in range(4):
        for sign in (1, -1):
            b_arrival(sign, 2, chunk, False)
        if chunk == 2:
            far_slabs(0, 6, 1)
    far_slabs(6, 2, 2)

    for c in range(3):
        cols = pl.ds(c * EDGE, EDGE)
        total = jnp.zeros((1, EDGE), jnp.float32)
        for r in range(4):
            rows = pl.ds(r * EDGE, EDGE)
            tile = acc[rows, cols]
            tile = jnp.where(keep_ref[r, c] != 0, tile * tile, jnp.zeros_like(tile))
            tiles[r * 3 + c] = tile
            total = total + jnp.sum(tile, axis=0, keepdims=True)
        sums[row, :, cols] = total

    def sum_copy(k, who):
        return pltpu.make_async_remote_copy(
            src_ref=sums.at[who], dst_ref=sums.at[who], send_sem=c_send.at[0], recv_sem=c_recv.at[0],
            device_id=(row_peer(k), col), device_id_type=MESH,
        )

    for k in range(7, 0, -1):
        sum_copy(k, row).start()
    for p in range(16):
        tile = tiles[slot_of[p]]
        slots[p] = jnp.where(filled[p] != 0, tile, jnp.zeros_like(tile))

    all_sums = pltpu.make_async_remote_copy(
        src_ref=sums.at[pl.ds(0, 7)], dst_ref=sums.at[pl.ds(0, 7)], send_sem=c_send.at[0], recv_sem=c_recv.at[0],
        device_id=(row_peer(1), col), device_id_type=MESH,
    )
    all_sums.wait_recv()

    total = sums[0]
    for i in range(1, 8):
        total = total + sums[i]
    scale = 1.0 / (total / (8 * 512) + 1e-5)
    for c in range(3):
        scales[c] = scale[:, c * EDGE:(c + 1) * EDGE]

    def fill(dest):
        for s in range(2):
            p = dest * 2 + s
            outgoing[dest, s] = (slots[p] * scales[third_of[p]]).astype(jnp.bfloat16)

    def move(k, who):
        return pltpu.make_async_remote_copy(
            src_ref=outgoing.at[row_peer(k)], dst_ref=moved_ref.at[who], send_sem=r_send.at[0], recv_sem=r_recv.at[0],
            device_id=(row_peer(k), col), device_id_type=MESH,
        )

    for k in range(7, 0, -1):
        fill(row_peer(k))
        move(k, row).start()
    fill(row)
    moved_ref[row] = outgoing[row]
    for r in range(4):
        for c in range(3):
            tile = tiles[r * 3 + c] * scale[:, c * EDGE:(c + 1) * EDGE]
            out_ref[pl.ds(r * EDGE, EDGE), pl.ds(c * EDGE, EDGE)] = tile.astype(jnp.bfloat16)

    def sent(ref, sem):
        pltpu.make_async_remote_copy(
            src_ref=ref, dst_ref=ref, send_sem=sem.at[0], recv_sem=r_recv.at[0], device_id=(row_peer(1), col), device_id_type=MESH
        ).wait_send()

    sent(a_all, a_send)
    pl.when(far >= 0)(lambda: sent(b_all.at[pl.ds(0, 1)], b_send))
    pl.when(far < 0)(lambda: sent(b_all.at[pl.ds(0, 5)], b_send))
    sent(b_all.at[pl.ds(0, 4)], s_send)
    all_sums.wait_send()
    every = pltpu.make_async_remote_copy(
        src_ref=outgoing.at[pl.ds(0, 7)], dst_ref=moved_ref.at[pl.ds(0, 7)], send_sem=r_send.at[0], recv_sem=r_recv.at[0],
        device_id=(row_peer(1), col), device_id_type=MESH,
    )
    every.wait_send()
    every.wait_recv()


def body(a, b, a_support, b_support, keep, bands):
    count = len(build_messages())
    dma = pltpu.SemaphoreType.DMA
    there = pl.BlockSpec(memory_space=pltpu.HBM)
    vmem = pl.BlockSpec(memory_space=pltpu.VMEM)
    out, moved = pl.pallas_call(
        kernel,
        out_shape=(
            jax.ShapeDtypeStruct((512, 384), jnp.bfloat16),
            jax.ShapeDtypeStruct((8, 2, EDGE, EDGE), jnp.bfloat16),
        ),
        in_specs=[there] * 6,
        out_specs=(vmem, vmem),
        scratch_shapes=[
            pltpu.VMEM((8, 2, 4, 512, EDGE), jnp.bfloat16),
            pltpu.VMEM((8, 1024, 384), jnp.bfloat16),
            pltpu.VMEM((512, 384), jnp.float32),
            pltpu.VMEM((12, EDGE, EDGE), jnp.float32),
            pltpu.VMEM((16, EDGE, EDGE), jnp.float32),
            pltpu.VMEM((3, 1, EDGE), jnp.float32),
            pltpu.VMEM((8, 2, EDGE, EDGE), jnp.bfloat16),
            pltpu.VMEM((8, 1, 384), jnp.float32),
            pltpu.VMEM((512, EDGE), jnp.bfloat16),
            pltpu.VMEM((512, EDGE), jnp.bfloat16),
            pltpu.VMEM((1024, 384), jnp.bfloat16),
            pltpu.SMEM((1, 4), jnp.int32),
            pltpu.SMEM((3, 8), jnp.int32),
            pltpu.SMEM((4, 3), jnp.int32),
            pltpu.SMEM((1, 12), jnp.int32),
            pltpu.SMEM((16,), jnp.int32),
            pltpu.SMEM((16,), jnp.int32),
            pltpu.SMEM((16,), jnp.int32),
            dma((1,)), dma((count,)), dma((16,)),
            dma((1,)), dma((2, 3, 4)),
            dma((1,)), dma((3,)),
            dma((2,)),
            dma((1,)), dma((1,)),
            dma((1,)), dma((1,)),
            dma((6,)),
        ],
        compiler_params=pltpu.CompilerParams(
            collective_id=0, has_side_effects=True, vmem_limit_bytes=40 * 1024 * 1024
        ),
        name="expand_and_move",
    )(*(pltpu.with_memory_space_constraint(v, pltpu.HBM) for v in (a, b, a_support.T, b_support.T, keep, bands.reshape(1, 12))))
    return out, moved.reshape(2048, EDGE)


def solution(mesh):
    split = P("row", "col")
    return jax.shard_map(
        body,
        mesh=mesh,
        in_specs=(split, split, split, split, split, P("row", "col", None, None)),
        out_specs=(split, split),
        check_vma=False,
    )
```

```python
import functools
import heapq

import jax
import jax.numpy as jnp
from jax import lax
from jax.experimental import pallas as pl
from jax.experimental.pallas import tpu as pltpu
from jax.sharding import PartitionSpec as P

MESH = pl.DeviceIdType.MESH
EDGE = 128
OWN, PARTNER = 0, 1
PARTS = {"full": (0, 512), "top": (0, 256), "bot": (256, 256)}
CHUNKS = ((0, 256), (256, 256), (512, 256), (768, 256))
BY_Z = ((1,), (1, 2))
PARTNER_READY = 9.0
BLOCK_US, HOP_US = 2.82, 1.8


def build_messages():
    msgs = []

    def add(axis, sign, dz, half, dx, part, level):
        came = (dz - sign, half, dx, part) if axis == "z" else (dz, half, dx - sign, part)
        msgs.append({"axis": axis, "sign": sign, "out": (dz, half, dx, part), "in": came, "level": level})

    for half in (OWN, PARTNER):
        for dx in (0, -1, 1, 2):
            for step in range(4):
                for sign in (1, -1):
                    if dx == 0 or step + 1 in BY_Z[half]:
                        part = "full" if step < 3 else ("top" if sign > 0 else "bot")
                        level = (0 if dx == 0 else 2) + step * 0.1
                        add("z", sign, -sign * step, half, dx, part, level)
        for dz in (0, -1, 1, -2, 2, -3, 3, 4):
            if abs(dz) not in BY_Z[half]:
                for sign in (1, -1):
                    add("x", sign, dz, half, 0, "full", abs(dz) * 0.1 + 0.5)
                for sign in (1, -1):
                    add("x", sign, dz, half, -sign, "top" if sign > 0 else "bot", abs(dz) * 0.1)
    return msgs


def halves(block):
    dz, half, dx, part = block
    key = (dz % 8, half, dx % 4)
    return {key + ("top",), key + ("bot",)} if part == "full" else {key + (part,)}


def group_of(m):
    return m["in"][0] % 8, m["in"][1]


def plan(msgs):
    source = {}
    for k, m in enumerate(msgs):
        for h in halves(m["in"]):
            source[h] = k
    needs = [{source[h] for h in halves(m["out"]) if h in source} for m in msgs]
    left = [set(n) for n in needs]
    links = [("x", 1), ("x", -1), ("z", 1), ("z", -1)]
    busy = {link: 0.0 for link in links}
    waiting = {link: [] for link in links}
    issued = {link: 0.0 for link in links}
    ready, arrived, starts = {}, {}, []
    events = []
    for k, m in enumerate(msgs):
        if not needs[k]:
            heapq.heappush(events, (PARTNER_READY if m["out"][1] == PARTNER else 0.0, 0, k))
    while events:
        t, kind, k = heapq.heappop(events)
        touched = links
        if kind == 0:
            m = msgs[k]
            ready[k] = t
            touched = [(m["axis"], m["sign"])]
            heapq.heappush(waiting[touched[0]], (m["level"], k))
        elif kind == 2:
            for n, rest in enumerate(left):
                if k in rest:
                    rest.discard(k)
                    if not rest:
                        heapq.heappush(events, (t, 0, n))
        for link in touched:
            if busy[link] <= t and waiting[link]:
                n = heapq.heappop(waiting[link])[1]
                busy[link] = t + PARTS[msgs[n]["out"][3]][1] / 512 * BLOCK_US
                arrived[n] = busy[link] + HOP_US
                issued[link] = max(issued[link], ready[n])
                starts.append((issued[link], n))
                heapq.heappush(events, (busy[link], 1, n))
                heapq.heappush(events, (arrived[n], 2, n))
    starts.sort(key=lambda e: e[0])
    relayed = set().union(*needs)
    waited = set()
    steps = []
    for t, k in starts:
        for n in sorted(needs[k], key=lambda i: arrived[i]):
            if n not in waited:
                waited.add(n)
                steps.append((t, "wait", n))
        if msgs[k]["out"][1] == PARTNER and "partner" not in waited:
            waited.add("partner")
            steps.append((t, "partner", 0))
        steps.append((t, "start", k))
    groups = {}
    for k, m in enumerate(msgs):
        if k not in relayed:
            groups.setdefault(group_of(m), []).append(k)
    for g, members in groups.items():
        steps.append((max(arrived[k] for k in members), "group", g))
    steps.sort(key=lambda e: e[0])
    return steps, sorted(groups), relayed


def kernel(
    a_hbm, b_hbm, asup_hbm, bsup_hbm, keep_hbm, band_hbm,
    out_ref, moved_ref,
    a_all, b_all, acc, tiles, slots, scales, outgoing, sums, relay, a_in, b_in,
    asup_ref, bsup_ref, keep_ref, band_ref, slot_of, filled, third_of,
    a_send, a_recv, g_recv, b_send, b_recv, s_send, s_recv, h_recv, c_send, c_recv, r_send, r_recv, local_sem,
):
    row, col = lax.axis_index("row"), lax.axis_index("col")
    y, core = row // 2, row % 2
    z, yh, x = col // 8, (col // 4) % 2, col % 4
    msgs = build_messages()
    steps, groups, relayed = plan(msgs)

    def row_peer(k):
        py = (3 - y, (y + 2) % 4, y + 1 - 2 * (y % 2), y)[3 - k // 2]
        pc = 1 - core if k % 2 else core
        return py * 2 + pc

    def col_at(dz, dx, half):
        h = yh if half == OWN else 1 - yh
        return ((z + dz + 8) % 8) * 8 + h * 4 + (x + dx + 4) % 4

    across = ((y + 2) % 4) * 2 + core
    neighbours = [(row, col_at(0, 1, OWN)), (row, col_at(0, -1, OWN)), (row, col_at(1, 0, OWN)), (row, col_at(-1, 0, OWN))]
    neighbours += [(row_peer(k), col) for k in range(1, 8)]
    neighbours.append((across, col_at(0, 0, PARTNER)))

    barrier = pltpu.get_barrier_semaphore()
    for device in neighbours:
        pl.semaphore_signal(barrier, inc=1, device_id=device, device_id_type=MESH)

    loads = [
        pltpu.make_async_copy(src, dst, local_sem.at[k])
        for k, (src, dst) in enumerate(
            ((asup_hbm, asup_ref), (a_hbm, a_in), (bsup_hbm, bsup_ref), (b_hbm, b_in), (keep_hbm, keep_ref), (band_hbm, band_ref))
        )
    ]
    for load in loads:
        load.start()

    loads[0].wait()
    loads[1].wait()
    for r in range(4):
        rows = pl.ds(r * EDGE, EDGE)
        tile = a_in[rows, :]
        a_all[z, yh, x, rows, :] = jnp.where(asup_ref[0, r] != 0, tile, jnp.zeros_like(tile))

    pl.semaphore_wait(barrier, len(neighbours))

    def block(spec):
        dz, half, dx, part = spec
        first, count = PARTS[part]
        h = yh if half == OWN else 1 - yh
        return a_all.at[(z + dz + 8) % 8, h, (x + dx + 4) % 4, pl.ds(first, count), :]

    def a_copy(k, spec):
        m = msgs[k]
        to = col_at(m["sign"], 0, OWN) if m["axis"] == "z" else col_at(0, m["sign"], OWN)
        return pltpu.make_async_remote_copy(
            src_ref=block(spec), dst_ref=block(spec), send_sem=a_send.at[0], recv_sem=a_recv.at[k] if k in relayed else g_recv.at[groups.index(group_of(m))],
            device_id=(row, to), device_id_type=MESH,
        )

    def group_arrived(g):
        dz, half = g
        size = sum(1 if m["in"][3] == "full" else 0.5 for k, m in enumerate(msgs) if k not in relayed and group_of(m) == g)
        ref = a_all.at[(z + dz) % 8, yh if half == OWN else 1 - yh, pl.ds(0, int(size))]
        pltpu.make_async_remote_copy(
            src_ref=ref, dst_ref=ref, send_sem=a_send.at[0], recv_sem=g_recv.at[groups.index(g)],
            device_id=(row, col_at(1, 0, OWN)), device_id_type=MESH,
        ).wait_recv()

    def half_copy(hop):
        if hop == 0:
            src, dst, to = a_all.at[z, yh, x], relay, (across, col)
        else:
            src, dst, to = relay, a_all.at[z, yh, x], (across, col_at(0, 0, PARTNER))
        return pltpu.make_async_remote_copy(
            src_ref=src, dst_ref=dst, send_sem=a_send.at[0], recv_sem=h_recv.at[hop], device_id=to, device_id_type=MESH
        )

    def half_arrival():
        dst = a_all.at[z, 1 - yh, x]
        return pltpu.make_async_remote_copy(
            src_ref=dst, dst_ref=dst, send_sem=a_send.at[0], recv_sem=h_recv.at[1],
            device_id=(across, col_at(0, 0, PARTNER)), device_id_type=MESH,
        )

    def b_slab(py, pc, chunk):
        first, count = CHUNKS[chunk]
        return b_all.at[py * 2 + pc, pl.ds(first, count), :]

    def b_copy(sign, d, chunk, py):
        way = 0 if sign > 0 else 1
        return pltpu.make_async_remote_copy(
            src_ref=b_slab(py, core, chunk), dst_ref=b_slab(py, core, chunk),
            send_sem=b_send.at[0], recv_sem=b_recv.at[way, d, chunk],
            device_id=((y + sign) * 2 + core, col), device_id_type=MESH,
        )

    def sends(sign, d):
        return (y >= d) & (y <= 2) if sign > 0 else (y + d <= 3) & (y >= 1)

    def receives(sign, d):
        return y >= 1 + d if sign > 0 else y + 1 + d <= 3

    def relays(sign, d):
        return receives(sign, d) & (y <= 2 if sign > 0 else y >= 1)

    def ends(sign, d):
        return receives(sign, d) & (y == 3 if sign > 0 else y == 0)

    def sibling_copy(kind, chunk, py, pc):
        return pltpu.make_async_remote_copy(
            src_ref=b_slab(py, pc, chunk), dst_ref=b_slab(py, pc, chunk),
            send_sem=s_send.at[0], recv_sem=s_recv.at[(2 if chunk == 3 else 1) if kind in (3, 6) else 0],
            device_id=(y * 2 + 1 - core, col), device_id_type=MESH,
        )

    def kind_of(sign, d):
        return 1 + d if sign > 0 else 4 + d

    def b_own(sign, chunk):
        @pl.when(sends(sign, 0))
        def _():
            b_copy(sign, 0, chunk, y).start()

    def b_arrival(sign, d, chunk, forward):
        @pl.when(relays(sign, d) if forward else ends(sign, d))
        def _():
            py = y - sign * (1 + d)
            b_copy(sign, d, chunk, py).wait_recv()
            if forward:
                b_copy(sign, d + 1, chunk, py).start()
            sibling_copy(kind_of(sign, d), chunk, py, core).start()

    half_copy(0).start()
    for k, m in enumerate(msgs):
        if m["out"] == (0, OWN, 0, "full"):
            a_copy(k, m["out"]).start()
    loads[2].wait()
    loads[3].wait()
    for r in range(8):
        for c in range(3):
            rows, cols = pl.ds(r * EDGE, EDGE), pl.ds(c * EDGE, EDGE)
            tile = b_in[rows, cols]
            b_all[row, rows, cols] = jnp.where(bsup_ref[c, r] != 0, tile, jnp.zeros_like(tile))
    for sign in (1, -1):
        b_own(sign, 0)
    half_copy(0).wait_recv()
    half_copy(1).start()
    for chunk in range(1, 4):
        for sign in (1, -1):
            b_own(sign, chunk)
    for chunk in range(4):
        sibling_copy(0, chunk, y, core).start()
    loads[4].wait()
    loads[5].wait()

    bands = [band_ref[0, t] for t in range(12)]
    places = []
    for t in range(12):
        rank = jnp.int32(0)
        for u in range(t):
            rank = rank + jnp.where(bands[u] == bands[t], 1, 0)
        places.append(bands[t] * 2 + rank)
    for p in range(16):
        which, any_of = jnp.int32(0), jnp.int32(0)
        for t in range(12):
            hit = places[t] == p
            which = jnp.where(hit, t, which)
            any_of = jnp.where(hit, 1, any_of)
        slot_of[p] = which
        third_of[p] = which % 3
        filled[p] = any_of

    far = jnp.where(y == 0, 3, jnp.where(y == 3, 0, -1))

    def multiply(slab, first=0, count=8):
        left = jnp.concatenate([a_all[slab, k // 4, k % 4] for k in range(first, first + count)], axis=1)
        right = b_all[slab, pl.ds(first * EDGE, count * EDGE), :]
        acc[...] += jnp.dot(left, right, preferred_element_type=jnp.float32)

    def early(dz):
        slab = (z + dz + 8) % 8

        @pl.when(slab // 2 != far)
        def _():
            multiply(slab)

    def siblings_arrived(ref, group):
        pltpu.make_async_remote_copy(
            src_ref=ref, dst_ref=ref, send_sem=s_send.at[0], recv_sem=s_recv.at[group],
            device_id=(y * 2 + 1 - core, col), device_id_type=MESH,
        ).wait_recv()

    def early_siblings():
        pl.when(far >= 0)(lambda: siblings_arrived(b_all.at[pl.ds(0, 3)], 0))
        pl.when(far < 0)(lambda: siblings_arrived(b_all.at[pl.ds(0, 4)], 0))

    acc[...] = jnp.zeros_like(acc)

    extra = []
    for d in range(2):
        for chunk in range(4):
            for sign in (1, -1):
                extra.append((17.0 * d + 4.25 * chunk + 14.5, functools.partial(b_arrival, sign, d, chunk, True)))
    for d, late in ((0, 33.0), (1, 45.5)):
        for chunk in range(4):
            for sign in (1, -1):
                extra.append((late, functools.partial(b_arrival, sign, d, chunk, False)))
    extra.append((46.3, early_siblings))
    for late, dz in ((46.31, 0), (46.32, -1), (46.33, 1), (46.34, -3), (47.75, 3), (48.8, -2), (48.81, 2), (99.0, 4)):
        extra.append((late, functools.partial(early, dz)))
    extra.sort(key=lambda e: e[0])
    for t, what, k in steps:
        while extra and extra[0][0] <= t:
            extra.pop(0)[1]()
        if what == "wait":
            a_copy(k, msgs[k]["in"]).wait_recv()
        elif what == "group":
            group_arrived(k)
        elif what == "partner":
            half_arrival().wait_recv()
        elif msgs[k]["out"] != (0, OWN, 0, "full"):
            a_copy(k, msgs[k]["out"]).start()
    for _, act in extra:
        act()

    def far_slabs(first, count, group):
        def more(i, carry):
            pl.when(i == 1)(lambda: siblings_arrived(b_all.at[0, pl.ds(0, count * EDGE)], group))
            multiply(far * 2 + (core + i) % 2, first, count)
            return carry

        @pl.when(far >= 0)
        def _():
            lax.fori_loop(0, 2, more, 0)

    for chunk in range(4):
        for sign in (1, -1):
            b_arrival(sign, 2, chunk, False)
        if chunk == 2:
            far_slabs(0, 6, 1)
    far_slabs(6, 2, 2)

    for c in range(3):
        cols = pl.ds(c * EDGE, EDGE)
        total = jnp.zeros((1, EDGE), jnp.float32)
        for r in range(4):
            rows = pl.ds(r * EDGE, EDGE)
            tile = acc[rows, cols]
            tile = jnp.where(keep_ref[r, c] != 0, tile * tile, jnp.zeros_like(tile))
            tiles[r * 3 + c] = tile
            total = total + jnp.sum(tile, axis=0, keepdims=True)
        sums[row, :, cols] = total

    def sum_copy(k, who):
        return pltpu.make_async_remote_copy(
            src_ref=sums.at[who], dst_ref=sums.at[who], send_sem=c_send.at[0], recv_sem=c_recv.at[0],
            device_id=(row_peer(k), col), device_id_type=MESH,
        )

    for k in range(7, 0, -1):
        sum_copy(k, row).start()
    for p in range(16):
        tile = tiles[slot_of[p]]
        slots[p] = jnp.where(filled[p] != 0, tile, jnp.zeros_like(tile))

    all_sums = pltpu.make_async_remote_copy(
        src_ref=sums.at[pl.ds(0, 7)], dst_ref=sums.at[pl.ds(0, 7)], send_sem=c_send.at[0], recv_sem=c_recv.at[0],
        device_id=(row_peer(1), col), device_id_type=MESH,
    )
    all_sums.wait_recv()

    total = sums[0]
    for i in range(1, 8):
        total = total + sums[i]
    scale = 1.0 / (total / (8 * 512) + 1e-5)
    for c in range(3):
        scales[c] = scale[:, c * EDGE:(c + 1) * EDGE]

    def fill(dest):
        for s in range(2):
            p = dest * 2 + s
            outgoing[dest, s] = (slots[p] * scales[third_of[p]]).astype(jnp.bfloat16)

    def move(k, who):
        return pltpu.make_async_remote_copy(
            src_ref=outgoing.at[row_peer(k)], dst_ref=moved_ref.at[who], send_sem=r_send.at[0], recv_sem=r_recv.at[0],
            device_id=(row_peer(k), col), device_id_type=MESH,
        )

    for k in range(7, 0, -1):
        fill(row_peer(k))
        move(k, row).start()
    fill(row)
    moved_ref[row] = outgoing[row]
    for r in range(4):
        for c in range(3):
            tile = tiles[r * 3 + c] * scale[:, c * EDGE:(c + 1) * EDGE]
            out_ref[pl.ds(r * EDGE, EDGE), pl.ds(c * EDGE, EDGE)] = tile.astype(jnp.bfloat16)

    def sent(ref, sem):
        pltpu.make_async_remote_copy(
            src_ref=ref, dst_ref=ref, send_sem=sem.at[0], recv_sem=r_recv.at[0], device_id=(row_peer(1), col), device_id_type=MESH
        ).wait_send()

    sent(a_all, a_send)
    pl.when(far >= 0)(lambda: sent(b_all.at[pl.ds(0, 1)], b_send))
    pl.when(far < 0)(lambda: sent(b_all.at[pl.ds(0, 5)], b_send))
    sent(b_all.at[pl.ds(0, 4)], s_send)
    all_sums.wait_send()
    every = pltpu.make_async_remote_copy(
        src_ref=outgoing.at[pl.ds(0, 7)], dst_ref=moved_ref.at[pl.ds(0, 7)], send_sem=r_send.at[0], recv_sem=r_recv.at[0],
        device_id=(row_peer(1), col), device_id_type=MESH,
    )
    every.wait_send()
    every.wait_recv()


def body(a, b, a_support, b_support, keep, bands):
    count = len(build_messages())
    dma = pltpu.SemaphoreType.DMA
    there = pl.BlockSpec(memory_space=pltpu.HBM)
    vmem = pl.BlockSpec(memory_space=pltpu.VMEM)
    out, moved = pl.pallas_call(
        kernel,
        out_shape=(
            jax.ShapeDtypeStruct((512, 384), jnp.bfloat16),
            jax.ShapeDtypeStruct((8, 2, EDGE, EDGE), jnp.bfloat16),
        ),
        in_specs=[there] * 6,
        out_specs=(vmem, vmem),
        scratch_shapes=[
            pltpu.VMEM((8, 2, 4, 512, EDGE), jnp.bfloat16),
            pltpu.VMEM((8, 1024, 384), jnp.bfloat16),
            pltpu.VMEM((512, 384), jnp.float32),
            pltpu.VMEM((12, EDGE, EDGE), jnp.float32),
            pltpu.VMEM((16, EDGE, EDGE), jnp.float32),
            pltpu.VMEM((3, 1, EDGE), jnp.float32),
            pltpu.VMEM((8, 2, EDGE, EDGE), jnp.bfloat16),
            pltpu.VMEM((8, 1, 384), jnp.float32),
            pltpu.VMEM((512, EDGE), jnp.bfloat16),
            pltpu.VMEM((512, EDGE), jnp.bfloat16),
            pltpu.VMEM((1024, 384), jnp.bfloat16),
            pltpu.SMEM((1, 4), jnp.int32),
            pltpu.SMEM((3, 8), jnp.int32),
            pltpu.SMEM((4, 3), jnp.int32),
            pltpu.SMEM((1, 12), jnp.int32),
            pltpu.SMEM((16,), jnp.int32),
            pltpu.SMEM((16,), jnp.int32),
            pltpu.SMEM((16,), jnp.int32),
            dma((1,)), dma((count,)), dma((16,)),
            dma((1,)), dma((2, 3, 4)),
            dma((1,)), dma((3,)),
            dma((2,)),
            dma((1,)), dma((1,)),
            dma((1,)), dma((1,)),
            dma((6,)),
        ],
        compiler_params=pltpu.CompilerParams(
            collective_id=0, has_side_effects=True, vmem_limit_bytes=40 * 1024 * 1024
        ),
        name="expand_and_move",
    )(*(pltpu.with_memory_space_constraint(v, pltpu.HBM) for v in (a, b, a_support.T, b_support.T, keep, bands.reshape(1, 12))))
    return out, moved.reshape(2048, EDGE)


def solution(mesh):
    split = P("row", "col")
    return jax.shard_map(
        body,
        mesh=mesh,
        in_specs=(split, split, split, split, split, P("row", "col", None, None)),
        out_specs=(split, split),
        check_vma=False,
    )
```

```python
import functools
import heapq

import jax
import jax.numpy as jnp
from jax import lax
from jax.experimental import pallas as pl
from jax.experimental.pallas import tpu as pltpu
from jax.sharding import PartitionSpec as P

MESH = pl.DeviceIdType.MESH
EDGE = 128
OWN, PARTNER = 0, 1
PARTS = {"full": (0, 512), "top": (0, 256), "bot": (256, 256)}
CHUNKS = ((0, 256), (256, 256), (512, 256), (768, 256))
BY_Z = ((1,), (1, 2))
PARTNER_READY = 10.0
BLOCK_US, HOP_US = 2.82, 1.8


def build_messages():
    msgs = []

    def add(axis, sign, dz, half, dx, part, level):
        came = (dz - sign, half, dx, part) if axis == "z" else (dz, half, dx - sign, part)
        msgs.append({"axis": axis, "sign": sign, "out": (dz, half, dx, part), "in": came, "level": level})

    for half in (OWN, PARTNER):
        for dx in (0, -1, 1, 2):
            for step in range(4):
                for sign in (1, -1):
                    if dx == 0 or step + 1 in BY_Z[half]:
                        part = "full" if step < 3 else ("top" if sign > 0 else "bot")
                        level = (0 if dx == 0 else 2) + step * 0.1
                        add("z", sign, -sign * step, half, dx, part, level)
        for dz in (0, -1, 1, -2, 2, -3, 3, 4):
            if abs(dz) not in BY_Z[half]:
                for sign in (1, -1):
                    add("x", sign, dz, half, 0, "full", abs(dz) * 0.1 + 0.5)
                for sign in (1, -1):
                    add("x", sign, dz, half, -sign, "top" if sign > 0 else "bot", abs(dz) * 0.1)
    return msgs


def halves(block):
    dz, half, dx, part = block
    key = (dz % 8, half, dx % 4)
    return {key + ("top",), key + ("bot",)} if part == "full" else {key + (part,)}


def group_of(m):
    return m["in"][0] % 8, m["in"][1]


def plan(msgs):
    source = {}
    for k, m in enumerate(msgs):
        for h in halves(m["in"]):
            source[h] = k
    needs = [{source[h] for h in halves(m["out"]) if h in source} for m in msgs]
    left = [set(n) for n in needs]
    links = [("x", 1), ("x", -1), ("z", 1), ("z", -1)]
    busy = {link: 0.0 for link in links}
    waiting = {link: [] for link in links}
    issued = {link: 0.0 for link in links}
    ready, arrived, starts = {}, {}, []
    events = []
    for k, m in enumerate(msgs):
        if not needs[k]:
            heapq.heappush(events, (PARTNER_READY if m["out"][1] == PARTNER else 0.0, 0, k))
    while events:
        t, kind, k = heapq.heappop(events)
        touched = links
        if kind == 0:
            m = msgs[k]
            ready[k] = t
            touched = [(m["axis"], m["sign"])]
            heapq.heappush(waiting[touched[0]], (m["level"], k))
        elif kind == 2:
            for n, rest in enumerate(left):
                if k in rest:
                    rest.discard(k)
                    if not rest:
                        heapq.heappush(events, (t, 0, n))
        for link in touched:
            if busy[link] <= t and waiting[link]:
                n = heapq.heappop(waiting[link])[1]
                busy[link] = t + PARTS[msgs[n]["out"][3]][1] / 512 * BLOCK_US
                arrived[n] = busy[link] + HOP_US
                issued[link] = max(issued[link], ready[n])
                starts.append((issued[link], n))
                heapq.heappush(events, (busy[link], 1, n))
                heapq.heappush(events, (arrived[n], 2, n))
    starts.sort(key=lambda e: e[0])
    relayed = set().union(*needs)
    waited = set()
    steps = []
    for t, k in starts:
        for n in sorted(needs[k], key=lambda i: arrived[i]):
            if n not in waited:
                waited.add(n)
                steps.append((t, "wait", n))
        if msgs[k]["out"][1] == PARTNER and "partner" not in waited:
            waited.add("partner")
            steps.append((t, "partner", 0))
        steps.append((t, "start", k))
    groups = {}
    for k, m in enumerate(msgs):
        if k not in relayed:
            groups.setdefault(group_of(m), []).append(k)
    for g, members in groups.items():
        steps.append((max(arrived[k] for k in members), "group", g))
    steps.sort(key=lambda e: e[0])
    return steps, sorted(groups), relayed


def kernel(
    a_hbm, b_hbm, asup_hbm, bsup_hbm, keep_hbm, band_hbm,
    out_ref, moved_ref,
    a_all, b_all, acc, tiles, slots, scales, outgoing, sums, relay, a_in, b_in,
    asup_ref, bsup_ref, keep_ref, band_ref, slot_of, filled, third_of,
    a_send, a_recv, g_recv, b_send, b_recv, s_send, s_recv, h_recv, c_send, c_recv, r_send, r_recv, local_sem,
):
    row, col = lax.axis_index("row"), lax.axis_index("col")
    y, core = row // 2, row % 2
    z, yh, x = col // 8, (col // 4) % 2, col % 4
    msgs = build_messages()
    steps, groups, relayed = plan(msgs)

    def row_peer(k):
        py = (3 - y, (y + 2) % 4, y + 1 - 2 * (y % 2), y)[3 - k // 2]
        pc = 1 - core if k % 2 else core
        return py * 2 + pc

    def col_at(dz, dx, half):
        h = yh if half == OWN else 1 - yh
        return ((z + dz + 8) % 8) * 8 + h * 4 + (x + dx + 4) % 4

    across = ((y + 2) % 4) * 2 + core
    neighbours = [(row, col_at(0, 1, OWN)), (row, col_at(0, -1, OWN)), (row, col_at(1, 0, OWN)), (row, col_at(-1, 0, OWN))]
    neighbours += [(row_peer(k), col) for k in range(1, 8)]
    neighbours.append((across, col_at(0, 0, PARTNER)))

    barrier = pltpu.get_barrier_semaphore()
    for device in neighbours:
        pl.semaphore_signal(barrier, inc=1, device_id=device, device_id_type=MESH)

    loads = [
        pltpu.make_async_copy(src, dst, local_sem.at[k])
        for k, (src, dst) in enumerate(
            ((asup_hbm, asup_ref), (a_hbm, a_in), (bsup_hbm, bsup_ref), (b_hbm, b_in), (keep_hbm, keep_ref), (band_hbm, band_ref))
        )
    ]
    for load in loads:
        load.start()

    loads[0].wait()
    loads[1].wait()
    for r in range(4):
        rows = pl.ds(r * EDGE, EDGE)
        tile = a_in[rows, :]
        a_all[z, yh, x, rows, :] = jnp.where(asup_ref[0, r] != 0, tile, jnp.zeros_like(tile))

    pl.semaphore_wait(barrier, len(neighbours))

    def block(spec):
        dz, half, dx, part = spec
        first, count = PARTS[part]
        h = yh if half == OWN else 1 - yh
        return a_all.at[(z + dz + 8) % 8, h, (x + dx + 4) % 4, pl.ds(first, count), :]

    def a_copy(k, spec):
        m = msgs[k]
        to = col_at(m["sign"], 0, OWN) if m["axis"] == "z" else col_at(0, m["sign"], OWN)
        return pltpu.make_async_remote_copy(
            src_ref=block(spec), dst_ref=block(spec), send_sem=a_send.at[0], recv_sem=a_recv.at[k] if k in relayed else g_recv.at[groups.index(group_of(m))],
            device_id=(row, to), device_id_type=MESH,
        )

    def group_arrived(g):
        dz, half = g
        size = sum(1 if m["in"][3] == "full" else 0.5 for k, m in enumerate(msgs) if k not in relayed and group_of(m) == g)
        ref = a_all.at[(z + dz) % 8, yh if half == OWN else 1 - yh, pl.ds(0, int(size))]
        pltpu.make_async_remote_copy(
            src_ref=ref, dst_ref=ref, send_sem=a_send.at[0], recv_sem=g_recv.at[groups.index(g)],
            device_id=(row, col_at(1, 0, OWN)), device_id_type=MESH,
        ).wait_recv()

    def half_copy(hop):
        if hop == 0:
            src, dst, to = a_all.at[z, yh, x], relay, (across, col)
        else:
            src, dst, to = relay, a_all.at[z, yh, x], (across, col_at(0, 0, PARTNER))
        return pltpu.make_async_remote_copy(
            src_ref=src, dst_ref=dst, send_sem=a_send.at[0], recv_sem=h_recv.at[hop], device_id=to, device_id_type=MESH
        )

    def half_arrival():
        dst = a_all.at[z, 1 - yh, x]
        return pltpu.make_async_remote_copy(
            src_ref=dst, dst_ref=dst, send_sem=a_send.at[0], recv_sem=h_recv.at[1],
            device_id=(across, col_at(0, 0, PARTNER)), device_id_type=MESH,
        )

    def b_slab(py, pc, chunk):
        first, count = CHUNKS[chunk]
        return b_all.at[py * 2 + pc, pl.ds(first, count), :]

    def b_copy(sign, d, chunk, py):
        way = 0 if sign > 0 else 1
        return pltpu.make_async_remote_copy(
            src_ref=b_slab(py, core, chunk), dst_ref=b_slab(py, core, chunk),
            send_sem=b_send.at[0], recv_sem=b_recv.at[way, d, chunk],
            device_id=((y + sign) * 2 + core, col), device_id_type=MESH,
        )

    def sends(sign, d):
        return (y >= d) & (y <= 2) if sign > 0 else (y + d <= 3) & (y >= 1)

    def receives(sign, d):
        return y >= 1 + d if sign > 0 else y + 1 + d <= 3

    def relays(sign, d):
        return receives(sign, d) & (y <= 2 if sign > 0 else y >= 1)

    def ends(sign, d):
        return receives(sign, d) & (y == 3 if sign > 0 else y == 0)

    def sibling_copy(kind, chunk, py, pc):
        return pltpu.make_async_remote_copy(
            src_ref=b_slab(py, pc, chunk), dst_ref=b_slab(py, pc, chunk),
            send_sem=s_send.at[0], recv_sem=s_recv.at[(2 if chunk == 3 else 1) if kind in (3, 6) else 0],
            device_id=(y * 2 + 1 - core, col), device_id_type=MESH,
        )

    def kind_of(sign, d):
        return 1 + d if sign > 0 else 4 + d

    def b_own(sign, chunk):
        @pl.when(sends(sign, 0))
        def _():
            b_copy(sign, 0, chunk, y).start()

    def b_arrival(sign, d, chunk, forward):
        @pl.when(relays(sign, d) if forward else ends(sign, d))
        def _():
            py = y - sign * (1 + d)
            b_copy(sign, d, chunk, py).wait_recv()
            if forward:
                b_copy(sign, d + 1, chunk, py).start()
            sibling_copy(kind_of(sign, d), chunk, py, core).start()

    half_copy(0).start()
    for k, m in enumerate(msgs):
        if m["out"] == (0, OWN, 0, "full"):
            a_copy(k, m["out"]).start()
    loads[2].wait()
    loads[3].wait()
    for r in range(8):
        for c in range(3):
            rows, cols = pl.ds(r * EDGE, EDGE), pl.ds(c * EDGE, EDGE)
            tile = b_in[rows, cols]
            b_all[row, rows, cols] = jnp.where(bsup_ref[c, r] != 0, tile, jnp.zeros_like(tile))
    for sign in (1, -1):
        b_own(sign, 0)
    half_copy(0).wait_recv()
    half_copy(1).start()
    for chunk in range(1, 4):
        for sign in (1, -1):
            b_own(sign, chunk)
    for chunk in range(4):
        sibling_copy(0, chunk, y, core).start()
    loads[4].wait()
    loads[5].wait()

    bands = [band_ref[0, t] for t in range(12)]
    places = []
    for t in range(12):
        rank = jnp.int32(0)
        for u in range(t):
            rank = rank + jnp.where(bands[u] == bands[t], 1, 0)
        places.append(bands[t] * 2 + rank)
    for p in range(16):
        which, any_of = jnp.int32(0), jnp.int32(0)
        for t in range(12):
            hit = places[t] == p
            which = jnp.where(hit, t, which)
            any_of = jnp.where(hit, 1, any_of)
        slot_of[p] = which
        third_of[p] = which % 3
        filled[p] = any_of

    far = jnp.where(y == 0, 3, jnp.where(y == 3, 0, -1))

    def multiply(slab, first=0, count=8):
        left = jnp.concatenate([a_all[slab, k // 4, k % 4] for k in range(first, first + count)], axis=1)
        right = b_all[slab, pl.ds(first * EDGE, count * EDGE), :]
        acc[...] += jnp.dot(left, right, preferred_element_type=jnp.float32)

    def early(dz):
        slab = (z + dz + 8) % 8

        @pl.when(slab // 2 != far)
        def _():
            multiply(slab)

    def siblings_arrived(ref, group):
        pltpu.make_async_remote_copy(
            src_ref=ref, dst_ref=ref, send_sem=s_send.at[0], recv_sem=s_recv.at[group],
            device_id=(y * 2 + 1 - core, col), device_id_type=MESH,
        ).wait_recv()

    def early_siblings():
        pl.when(far >= 0)(lambda: siblings_arrived(b_all.at[pl.ds(0, 3)], 0))
        pl.when(far < 0)(lambda: siblings_arrived(b_all.at[pl.ds(0, 4)], 0))

    acc[...] = jnp.zeros_like(acc)

    extra = []
    for d in range(2):
        for chunk in range(4):
            for sign in (1, -1):
                extra.append((17.0 * d + 4.25 * chunk + 14.5, functools.partial(b_arrival, sign, d, chunk, True)))
    for d, late in ((0, 33.0), (1, 45.5)):
        for chunk in range(4):
            for sign in (1, -1):
                extra.append((late, functools.partial(b_arrival, sign, d, chunk, False)))
    extra.append((46.3, early_siblings))
    for late, dz in ((46.31, 0), (46.32, -1), (46.33, 1), (46.34, -3), (47.75, 3), (48.8, -2), (48.81, 2), (99.0, 4)):
        extra.append((late, functools.partial(early, dz)))
    extra.sort(key=lambda e: e[0])
    for t, what, k in steps:
        while extra and extra[0][0] <= t:
            extra.pop(0)[1]()
        if what == "wait":
            a_copy(k, msgs[k]["in"]).wait_recv()
        elif what == "group":
            group_arrived(k)
        elif what == "partner":
            half_arrival().wait_recv()
        elif msgs[k]["out"] != (0, OWN, 0, "full"):
            a_copy(k, msgs[k]["out"]).start()
    for _, act in extra:
        act()

    def far_slabs(first, count, group):
        def more(i, carry):
            pl.when(i == 1)(lambda: siblings_arrived(b_all.at[0, pl.ds(0, count * EDGE)], group))
            multiply(far * 2 + (core + i) % 2, first, count)
            return carry

        @pl.when(far >= 0)
        def _():
            lax.fori_loop(0, 2, more, 0)

    for chunk in range(4):
        for sign in (1, -1):
            b_arrival(sign, 2, chunk, False)
        if chunk == 2:
            far_slabs(0, 6, 1)
    far_slabs(6, 2, 2)

    for c in range(3):
        cols = pl.ds(c * EDGE, EDGE)
        total = jnp.zeros((1, EDGE), jnp.float32)
        for r in range(4):
            rows = pl.ds(r * EDGE, EDGE)
            tile = acc[rows, cols]
            tile = jnp.where(keep_ref[r, c] != 0, tile * tile, jnp.zeros_like(tile))
            tiles[r * 3 + c] = tile
            total = total + jnp.sum(tile, axis=0, keepdims=True)
        sums[row, :, cols] = total

    def sum_copy(k, who):
        return pltpu.make_async_remote_copy(
            src_ref=sums.at[who], dst_ref=sums.at[who], send_sem=c_send.at[0], recv_sem=c_recv.at[0],
            device_id=(row_peer(k), col), device_id_type=MESH,
        )

    for k in range(7, 0, -1):
        sum_copy(k, row).start()
    for p in range(16):
        tile = tiles[slot_of[p]]
        slots[p] = jnp.where(filled[p] != 0, tile, jnp.zeros_like(tile))

    all_sums = pltpu.make_async_remote_copy(
        src_ref=sums.at[pl.ds(0, 7)], dst_ref=sums.at[pl.ds(0, 7)], send_sem=c_send.at[0], recv_sem=c_recv.at[0],
        device_id=(row_peer(1), col), device_id_type=MESH,
    )
    all_sums.wait_recv()

    total = sums[0]
    for i in range(1, 8):
        total = total + sums[i]
    scale = 1.0 / (total / (8 * 512) + 1e-5)
    for c in range(3):
        scales[c] = scale[:, c * EDGE:(c + 1) * EDGE]

    def fill(dest):
        for s in range(2):
            p = dest * 2 + s
            outgoing[dest, s] = (slots[p] * scales[third_of[p]]).astype(jnp.bfloat16)

    def move(k, who):
        return pltpu.make_async_remote_copy(
            src_ref=outgoing.at[row_peer(k)], dst_ref=moved_ref.at[who], send_sem=r_send.at[0], recv_sem=r_recv.at[0],
            device_id=(row_peer(k), col), device_id_type=MESH,
        )

    for k in range(7, 0, -1):
        fill(row_peer(k))
        move(k, row).start()
    fill(row)
    moved_ref[row] = outgoing[row]
    for r in range(4):
        for c in range(3):
            tile = tiles[r * 3 + c] * scale[:, c * EDGE:(c + 1) * EDGE]
            out_ref[pl.ds(r * EDGE, EDGE), pl.ds(c * EDGE, EDGE)] = tile.astype(jnp.bfloat16)

    def sent(ref, sem):
        pltpu.make_async_remote_copy(
            src_ref=ref, dst_ref=ref, send_sem=sem.at[0], recv_sem=r_recv.at[0], device_id=(row_peer(1), col), device_id_type=MESH
        ).wait_send()

    sent(a_all, a_send)
    pl.when(far >= 0)(lambda: sent(b_all.at[pl.ds(0, 1)], b_send))
    pl.when(far < 0)(lambda: sent(b_all.at[pl.ds(0, 5)], b_send))
    sent(b_all.at[pl.ds(0, 4)], s_send)
    all_sums.wait_send()
    every = pltpu.make_async_remote_copy(
        src_ref=outgoing.at[pl.ds(0, 7)], dst_ref=moved_ref.at[pl.ds(0, 7)], send_sem=r_send.at[0], recv_sem=r_recv.at[0],
        device_id=(row_peer(1), col), device_id_type=MESH,
    )
    every.wait_send()
    every.wait_recv()


def body(a, b, a_support, b_support, keep, bands):
    count = len(build_messages())
    dma = pltpu.SemaphoreType.DMA
    there = pl.BlockSpec(memory_space=pltpu.HBM)
    vmem = pl.BlockSpec(memory_space=pltpu.VMEM)
    out, moved = pl.pallas_call(
        kernel,
        out_shape=(
            jax.ShapeDtypeStruct((512, 384), jnp.bfloat16),
            jax.ShapeDtypeStruct((8, 2, EDGE, EDGE), jnp.bfloat16),
        ),
        in_specs=[there] * 6,
        out_specs=(vmem, vmem),
        scratch_shapes=[
            pltpu.VMEM((8, 2, 4, 512, EDGE), jnp.bfloat16),
            pltpu.VMEM((8, 1024, 384), jnp.bfloat16),
            pltpu.VMEM((512, 384), jnp.float32),
            pltpu.VMEM((12, EDGE, EDGE), jnp.float32),
            pltpu.VMEM((16, EDGE, EDGE), jnp.float32),
            pltpu.VMEM((3, 1, EDGE), jnp.float32),
            pltpu.VMEM((8, 2, EDGE, EDGE), jnp.bfloat16),
            pltpu.VMEM((8, 1, 384), jnp.float32),
            pltpu.VMEM((512, EDGE), jnp.bfloat16),
            pltpu.VMEM((512, EDGE), jnp.bfloat16),
            pltpu.VMEM((1024, 384), jnp.bfloat16),
            pltpu.SMEM((1, 4), jnp.int32),
            pltpu.SMEM((3, 8), jnp.int32),
            pltpu.SMEM((4, 3), jnp.int32),
            pltpu.SMEM((1, 12), jnp.int32),
            pltpu.SMEM((16,), jnp.int32),
            pltpu.SMEM((16,), jnp.int32),
            pltpu.SMEM((16,), jnp.int32),
            dma((1,)), dma((count,)), dma((16,)),
            dma((1,)), dma((2, 3, 4)),
            dma((1,)), dma((3,)),
            dma((2,)),
            dma((1,)), dma((1,)),
            dma((1,)), dma((1,)),
            dma((6,)),
        ],
        compiler_params=pltpu.CompilerParams(
            collective_id=0, has_side_effects=True, vmem_limit_bytes=40 * 1024 * 1024
        ),
        name="expand_and_move",
    )(*(pltpu.with_memory_space_constraint(v, pltpu.HBM) for v in (a, b, a_support.T, b_support.T, keep, bands.reshape(1, 12))))
    return out, moved.reshape(2048, EDGE)


def solution(mesh):
    split = P("row", "col")
    return jax.shard_map(
        body,
        mesh=mesh,
        in_specs=(split, split, split, split, split, P("row", "col", None, None)),
        out_specs=(split, split),
        check_vma=False,
    )
```
